32 devices in a mesh: grp: 2 (over x), tile: 16 (over z, y, core).
Axes of the slice: x: 2, y: 2, z: 4, core: 2. Of those that a mesh axis runs over, the one named last changes fastest.
Arguments:
- state: bfloat16 [256, 16, 512], P(('grp', 'tile')), parts along dimension 0, may hold values from -36 to 36
- wet: int32 [128], replicated, may hold values from 0 to 1, as said below
- w_vqkv: bfloat16 [512, 1536], replicated, may hold values from -0.25 to 0.25
- w_vout: bfloat16 [512, 512], replicated, may hold values from -0.25 to 0.25
- w_hqkv: bfloat16 [512, 1536], replicated, may hold values from -0.25 to 0.25
- w_hout: bfloat16 [512, 512], replicated, may hold values from -0.25 to 0.25
Outputs:
- updated: bfloat16 [256, 16, 512], P(('grp', 'tile')), parts along dimension 0
The draws below stay inside these ranges and needn't reach their ends.
There are 2 independent parts, one for each index of `grp`. The reference program is written for one: setup_inputs(seed, part) draws one part's arguments, and reference() takes and returns one part's arrays. A program takes and returns all parts, laid end to end along the dimension named above; an argument that names none is the same for every part. Nothing has to cross between parts.
Inputs may be any that keep to these rules, and one draw needn't show every extreme that they name: For every strip s (blocks s * 8 to s * 8 + 7), exactly 1 of the 2 blocks with b mod 4 == 0 is wet, and exactly 1 of the 2 blocks with b mod 4 == 3.
All inputs are finite; a program needn't handle non-finite values.
Results may differ from the reference program's by a relative error of at most 0.007.
Values may be sent and summed in bfloat16 or wider, within the bound.
A program may use at most 64 MiB of HBM per device.

```python
import math
import jax
import jax.numpy as jnp
from jax import lax

D = 512
HEADS = 4
CB = 4
RB = 2
EDGE_WET = 1
TBLK = 8
LEV = 16
BLOCKS = 128
N_TILE = 16


def draw_state(key, part):
    key_base, key_rows, key_cols = jax.random.split(key, 3)
    row_scale = jnp.exp(jax.random.uniform(key_rows, (BLOCKS, LEV, 1), jnp.float32, math.log(0.3), math.log(3.0)))
    col_scale = jnp.exp(jax.random.uniform(key_cols, (1, 1, D), jnp.float32, math.log(0.3), math.log(3.0)))
    base = jnp.clip(jax.random.normal(key_base, (BLOCKS, LEV, D), jnp.float32), -4.0, 4.0)
    return (base * row_scale * col_scale).astype(jnp.bfloat16)


def draw_wet(key, part):
    key_inner, key_edge = jax.random.split(jax.random.fold_in(key, 17), 2)
    strips = BLOCKS // TBLK
    inner = (jax.random.randint(key_inner, (strips, RB, CB), 0, 4) < 3).astype(jnp.int32)
    raw = jax.random.randint(key_edge, (strips, 2, RB), 0, 1048576)
    scores = raw * RB + jnp.arange(RB, dtype=jnp.int32)[None, None, :]
    order = jnp.argsort(scores, axis=-1)
    ranks = jnp.argsort(order, axis=-1)
    edge = (ranks < EDGE_WET).astype(jnp.int32)
    column = jnp.arange(CB, dtype=jnp.int32)[None, None, :]
    result = jnp.where(column == 0, edge[:, 0, :, None], inner)
    result = jnp.where(column == CB - 1, edge[:, 1, :, None], result)
    return result.reshape(BLOCKS).astype(jnp.int32)


def bell_draw(stream_key, shape, width, bound, kind=jnp.bfloat16):
    array = jax.random.normal(stream_key, shape, jnp.float32) * width
    return jnp.minimum(jnp.maximum(array, -bound), bound).astype(kind)


def setup_inputs(seed: int = 0, part: int = 0) -> dict:
    arg_keys = jax.random.split(jax.random.key(seed), 7)
    part_splits = jax.random.split(jax.random.fold_in(arg_keys[6], part), 7)
    state = draw_state(jax.random.fold_in(jax.random.fold_in(arg_keys[6], part), 71), part)
    wet = draw_wet(jax.random.fold_in(arg_keys[6], 71), part)
    w_vqkv = bell_draw(arg_keys[2], (D, 3 * D), D ** -0.5, 0.25)
    w_vout = bell_draw(arg_keys[3], (D, D), D ** -0.5, 0.25)
    w_hqkv = bell_draw(arg_keys[4], (D, 3 * D), D ** -0.5, 0.25)
    w_hout = bell_draw(arg_keys[5], (D, D), D ** -0.5, 0.25)
    return dict(state=state, wet=wet, w_vqkv=w_vqkv, w_vout=w_vout, w_hqkv=w_hqkv, w_hout=w_hout)


EPSILON = 1e-06

def row_norm(values):
    values = values.astype(jnp.float32)
    return values * lax.rsqrt(lax.optimization_barrier(jnp.mean(values * values, axis=-1, keepdims=True)) + EPSILON)

def project(inputs, weights):
    feature_width = inputs.shape[-1]
    head_size = feature_width // HEADS
    normed = row_norm(inputs).astype(jnp.bfloat16)
    joined = jnp.dot(normed.reshape(-1, feature_width), weights, preferred_element_type=jnp.float32)
    target_shape = inputs.shape[:-1] + (HEADS, head_size)
    query = row_norm(joined[:, :feature_width].reshape(target_shape)).astype(jnp.bfloat16)
    keys = row_norm(joined[:, feature_width:2 * feature_width].reshape(target_shape)).astype(jnp.bfloat16)
    values = joined[:, 2 * feature_width:].reshape(target_shape).astype(jnp.bfloat16)
    return (query, keys, values)

def finish(inputs, context, weights):
    feature_width = inputs.shape[-1]
    update = jnp.dot(context.reshape(-1, feature_width), weights, preferred_element_type=jnp.float32)
    return (inputs.astype(jnp.float32) + update.reshape(inputs.shape)).astype(jnp.bfloat16)

def vertical_block(block, w_vqkv, w_vout):
    query, keys, values = project(block, w_vqkv)
    scale = 1.0 / math.sqrt(query.shape[-1])
    scores = jnp.einsum('clhd,cmhd->chlm', query.astype(jnp.float32), keys.astype(jnp.float32)) * scale
    expon = jnp.exp(scores)
    probs = (expon / lax.optimization_barrier(jnp.sum(expon, axis=-1, keepdims=True))).astype(jnp.bfloat16)
    context = jnp.einsum('chlm,cmhd->clhd', probs.astype(jnp.float32), values.astype(jnp.float32)).astype(jnp.bfloat16)
    return finish(block, context, w_vout)

def to_grid(blocks, tiles):
    rest = blocks.shape[1:]
    row_count = blocks.shape[0] // (tiles * CB)
    shaped = jnp.moveaxis(blocks.reshape((tiles, row_count, CB) + rest), 0, 1)
    return shaped.reshape((row_count, tiles * CB) + rest)

def from_grid(grid, tiles):
    rest = grid.shape[2:]
    row_count = grid.shape[0]
    shaped = jnp.moveaxis(grid.reshape((row_count, tiles, CB) + rest), 1, 0)
    return shaped.reshape((tiles * row_count * CB,) + rest)

def wrap_columns(grid):
    return jnp.concatenate([grid[:, -1:], grid, grid[:, :1]], axis=1)

def neighbour_mix(query, keys_ext, values_ext, wet_ext):
    row_count = query.shape[0]
    col_count = query.shape[1]
    scale = 1.0 / math.sqrt(query.shape[-1])
    padding = ((1, 1), (0, 0), (0, 0), (0, 0), (0, 0))
    keys_pad = jnp.pad(keys_ext, padding)
    values_pad = jnp.pad(values_ext, padding)
    wet_pad = jnp.pad(wet_ext, ((1, 1), (0, 0)))
    inside = jnp.pad(jnp.ones((row_count, col_count + 2), jnp.int32), ((1, 1), (0, 0)))
    query_f = query.astype(jnp.float32)
    weights_list = []
    values_list = []
    for row_step in (-1, 0, 1):
        for col_step in (-1, 0, 1):
            rows_here = slice(1 + row_step, 1 + row_step + row_count)
            cols_here = slice(1 + col_step, 1 + col_step + col_count)
            shifted = keys_pad[rows_here, cols_here].astype(jnp.float32)
            scores = lax.optimization_barrier(jnp.sum(query_f * shifted, axis=-1)) * scale
            if row_step == 0 and col_step == 0:
                allowed = jnp.ones((row_count, col_count), jnp.int32)
            else:
                allowed = inside[rows_here, cols_here] * wet_pad[rows_here, cols_here]
            weights_list.append(jnp.where(allowed[:, :, None, None] > 0, jnp.exp(scores), jnp.float32(0.0)))
            values_list.append(values_pad[rows_here, cols_here])
    total = weights_list[0]
    for extra in weights_list[1:]:
        total = total + extra
    context = jnp.zeros(query.shape, jnp.float32)
    for weight_now, value_now in zip(weights_list, values_list):
        probs = (weight_now / total).astype(jnp.bfloat16)
        context = context + probs.astype(jnp.float32)[..., None] * value_now.astype(jnp.float32)
    return context.astype(jnp.bfloat16)

def reference(state, wet, w_vqkv, w_vout, w_hqkv, w_hout):
    blocks_all = state.shape[0]
    levels = state.shape[1]
    feature_width = state.shape[2]
    strips = state.reshape(N_TILE, blocks_all // N_TILE, levels, feature_width)
    mixed = lax.map(lambda block: vertical_block(block, w_vqkv, w_vout), strips)
    mixed = mixed.reshape(blocks_all, levels, feature_width)
    wet_ext = wrap_columns(to_grid(wet, N_TILE))

    def level_step(level_rows):
        grid = to_grid(level_rows, N_TILE)[:, :, None]
        query, keys, values = project(grid, w_hqkv)
        context = neighbour_mix(query, wrap_columns(keys), wrap_columns(values), wet_ext)
        result = finish(grid, context, w_hout)
        return from_grid(result[:, :, 0], N_TILE)
    per_level = lax.map(level_step, jnp.swapaxes(mixed, 0, 1))
    return jnp.swapaxes(per_level, 0, 1)
```

```python
import functools
import math

import jax
import jax.numpy as jnp
from jax import lax
from jax.experimental import pallas as pl
from jax.experimental.pallas import tpu as pltpu
from jax.sharding import PartitionSpec as P

HEADS = 4
CB = 4
ROWS = 128
PARTS = 2
EPSILON = 1e-06
MESH = pl.DeviceIdType.MESH
BF16 = jnp.bfloat16
F32 = jnp.float32


def inverse_rms(values):
    return lax.rsqrt(jnp.mean(values * values, axis=-1, keepdims=True) + EPSILON)


def dot(a, b):
    return jnp.dot(a, b, preferred_element_type=F32)


def unit_heads(raw, factor):
    head = raw.shape[-1] // HEADS
    square = factor * factor
    out = []
    for h in range(HEADS):
        part = raw[:, h * head : (h + 1) * head]
        mean = jnp.mean(part * part, axis=-1, keepdims=True)
        out.append((part * (factor * lax.rsqrt(mean * square + EPSILON))).astype(BF16))
    return out


def value_heads(raw, factor):
    head = raw.shape[-1] // HEADS
    values = (raw * factor).astype(BF16)
    ones = jnp.ones((values.shape[0], head), BF16)
    return [
        jnp.concatenate([values[:, h * head : (h + 1) * head], ones], axis=1)
        for h in range(HEADS)
    ]


def weigh(query, keys, values, mask):
    parts = []
    for q, k, v in zip(query, keys, values):
        scale = 1.0 / math.sqrt(q.shape[-1])
        scores = lax.dot_general(q, k, (((1,), (1,)), ((), ())), preferred_element_type=F32)
        expon = jnp.where(mask, jnp.exp(scores * scale), 0.0).astype(BF16)
        parts.append(dot(expon, v))
    return parts


def contexts(parts):
    out = []
    for part in parts:
        head = part.shape[-1] // 2
        out.append((part[:, :head] / part[:, head:]).astype(BF16))
    return jnp.concatenate(out, axis=1)


def loop(count, body):
    if count == 1:
        body(0)
    else:
        lax.fori_loop(0, count, lambda i, c: (body(i), c)[1], 0)


def large_kernel(
    tiles,
    wet_hbm,
    state,
    w_vqkv,
    w_vout,
    w_hqkv,
    w_hout,
    out,
    wet,
    own,
    halo,
    mixed,
    vqkv,
    vout,
    hqkv,
    hout,
    sems,
    ready,
    send_sems,
    recv_sems,
):
    rows, cols, levels, width = state.shape
    blocks = rows * cols
    me = lax.axis_index("tile")
    right = lax.rem(me + 1, tiles)
    left = lax.rem(me + tiles - 1, tiles)

    barrier = pltpu.get_barrier_semaphore()
    pl.semaphore_signal(barrier, inc=1, device_id={"tile": left}, device_id_type=MESH)

    started = []

    def fetch(src, dst):
        copy = pltpu.make_async_copy(src, dst, sems.at[len(started)])
        copy.start()
        started.append(copy)
        return copy

    sends = [
        pltpu.make_async_remote_copy(
            src_ref=state.at[:, column],
            dst_ref=halo.at[i],
            send_sem=send_sems.at[i],
            recv_sem=recv_sems.at[i],
            device_id={"tile": side},
            device_id_type=MESH,
        )
        for i, (column, side) in enumerate(((cols - 1, right), (0, left)))
    ]

    def send_right():
        pl.semaphore_wait(barrier, 1)
        sends[0].start()
        pl.semaphore_signal(ready, inc=1, device_id={"tile": right}, device_id_type=MESH)

    def send_left():
        pl.semaphore_wait(ready, 1)
        sends[1].start()

    last = me == tiles - 1

    def send_first():
        send_right()
        sends[0].wait_send()

    pl.when(last)(send_first)
    get_state = [fetch(state.at[r], own.at[pl.ds(r * cols, cols)]) for r in range(rows)]
    get_vqkv = [fetch(w_vqkv.at[:, pl.ds(i * width, width)], vqkv.at[i]) for i in range(3)]
    pl.when(jnp.logical_not(last))(send_right)
    get_wet = fetch(wet_hbm, wet)
    get_vout = fetch(w_vout, vout)
    get_hqkv = [fetch(w_hqkv.at[:, pl.ds(i * width, width)], hqkv.at[i]) for i in range(3)]
    get_hout = fetch(w_hout, hout)

    def vertical(tokens):
        count = tokens.shape[0]
        values = tokens.astype(F32)
        factor = inverse_rms(values)
        joined = []
        for i in range(3):
            joined.append(dot(tokens, vqkv[i]))
        row = lax.broadcasted_iota(jnp.int32, (count, count), 0) // levels
        col = lax.broadcasted_iota(jnp.int32, (count, count), 1) // levels
        query, keys = unit_heads(joined[0], factor), unit_heads(joined[1], factor)
        context = contexts(weigh(query, keys, value_heads(joined[2], factor), row == col))
        return (values + dot(context, vout[...])).astype(BF16)

    group = max(1, min(blocks, ROWS // levels))
    for copy in get_state:
        copy.wait()
    pl.when(me != 0)(send_left)
    for copy in get_vqkv:
        copy.wait()
    get_vout.wait()

    def own_step(i):
        picked = pl.ds(i * group, group)
        tokens = own[picked].reshape(group * levels, width)
        mixed[picked] = vertical(tokens).reshape(group, levels, width)

    loop(blocks // group, own_step)

    pl.when(me == 0)(send_left)

    for copy in get_hqkv:
        copy.wait()
    get_wet.wait()

    step = min(levels, ROWS // blocks)
    n_own = blocks * step

    key_block = lax.broadcasted_iota(jnp.int32, (1, n_own), 1) // step
    wet_key = jnp.zeros((1, n_own), jnp.int32)
    for b in range(blocks):
        wet_key = jnp.where(key_block == b, wet[me * blocks + b], wet_key)
    row_id = lax.broadcasted_iota(jnp.int32, (n_own, n_own), 0)
    key_id = lax.broadcasted_iota(jnp.int32, (n_own, n_own), 1)
    near = jnp.abs(row_id // step % cols - key_id // step % cols) <= 1
    counted = jnp.logical_or(wet_key > 0, row_id // step == key_block)
    own_mask = (row_id % step == key_id % step) & near & counted

    edges = [r * cols + c for r in range(rows) for c in (0, cols - 1)]
    n_edge = len(edges) * step
    row_id = lax.broadcasted_iota(jnp.int32, (n_edge, 2 * step), 0)
    key_id = lax.broadcasted_iota(jnp.int32, (n_edge, 2 * step), 1)
    halo_mask = (row_id % step == key_id % step) & (row_id // step % 2 == key_id // step)

    def edge_rows(values):
        return jnp.concatenate([values[b * step : (b + 1) * step] for b in edges], axis=0)

    def inner_rows(values):
        spans = [((r * cols + 1) * step, (r * cols + cols - 1) * step) for r in range(rows)]
        return jnp.concatenate([values[first:end] for first, end in spans], axis=0)

    def among_own(i):
        picked = pl.ds(i * step, step)
        tokens = mixed[pl.ds(0, blocks), picked].reshape(n_own, width)
        values = tokens.astype(F32)
        factor = inverse_rms(values)
        query = unit_heads(dot(tokens, hqkv[0]), factor)
        keys = unit_heads(dot(tokens, hqkv[1]), factor)
        value = value_heads(dot(tokens, hqkv[2]), factor)
        parts = weigh(query, keys, value, own_mask)
        context = contexts([inner_rows(p) for p in parts])
        updated = (inner_rows(values) + dot(context, hout[...])).astype(BF16)
        updated = updated.reshape(rows, cols - 2, step, width)
        for r in range(rows):
            out[pl.ds(r * cols + 1, cols - 2), picked] = updated[r]
        query = [edge_rows(q) for q in query]
        return edge_rows(values), query, [edge_rows(p) for p in parts]

    def with_halo(i, beside, values, query, parts):
        picked = pl.ds(i * step, step)
        factor = inverse_rms(beside.astype(F32))
        keys = unit_heads(dot(beside, hqkv[1]), factor)
        value = value_heads(dot(beside, hqkv[2]), factor)
        more = weigh(query, keys, value, halo_mask)
        context = contexts([a + b for a, b in zip(parts, more)])
        updated = (values + dot(context, hout[...])).astype(BF16)
        for e, b in enumerate(edges):
            out[b, picked] = updated[e * step : (e + 1) * step]

    get_hout.wait()
    for i, copy in enumerate(sends):
        copy.wait_recv()
        block = (left * blocks + cols - 1, right * blocks)[i]
        picked_halo = jnp.where(wet[block] > 0, halo[i, 0], halo[i, 1])
        mixed[blocks + i] = vertical(picked_halo)

    def level_step(i):
        beside = mixed[pl.ds(blocks, 2), pl.ds(i * step, step)]
        with_halo(i, beside.reshape(2 * step, width), *among_own(i))

    loop(levels // step, level_step)
    pl.when(jnp.logical_not(last))(sends[0].wait_send)
    sends[1].wait_send()


def lanes(values, h):
    head = values.shape[-1] // HEADS
    return values[..., h * head : (h + 1) * head]


def square_means(values):
    return [jnp.mean(lanes(values, h) * lanes(values, h), axis=-1, keepdims=True) for h in range(HEADS)]


def small_kernel(
    tiles,
    wet_hbm,
    state,
    w_vqkv,
    w_vout,
    w_hqkv,
    w_hout,
    out,
    wet,
    own,
    halo,
    edge_base,
    edge_query,
    edge_total,
    edge_sum,
    vqkv,
    vout,
    hqkv,
    hout,
    sems,
    ready,
    send_sems,
    recv_sems,
):
    rows, cols, levels, width = state.shape
    blocks = rows * cols
    head = width // HEADS
    count = blocks * levels
    scale = 1.0 / math.sqrt(head)
    me = lax.axis_index("tile")
    right = lax.rem(me + 1, tiles)
    left = lax.rem(me + tiles - 1, tiles)
    last = me == tiles - 1

    barrier = pltpu.get_barrier_semaphore()
    pl.semaphore_signal(barrier, inc=1, device_id={"tile": left}, device_id_type=MESH)

    started = []

    def fetch(src, dst):
        copy = pltpu.make_async_copy(src, dst, sems.at[len(started)])
        copy.start()
        started.append(copy)
        return copy

    part = width // PARTS
    spans = [pl.ds(p * part, part) for p in range(PARTS)]

    def halo_copy(i, p, column, side):
        return pltpu.make_async_remote_copy(
            src_ref=state.at[:, column, :, spans[p]],
            dst_ref=halo.at[i, :, :, spans[p]],
            send_sem=send_sems.at[i, p],
            recv_sem=recv_sems.at[i, p],
            device_id={"tile": side},
            device_id_type=MESH,
        )

    rightward = [halo_copy(0, p, cols - 1, right) for p in range(PARTS)]
    leftward = [halo_copy(1, p, 0, left) for p in range(PARTS)]

    def send_right():
        pl.semaphore_wait(barrier, 1)
        for copy in rightward:
            copy.start()
        pl.semaphore_signal(ready, inc=1, device_id={"tile": right}, device_id_type=MESH)

    def send_left():
        pl.semaphore_wait(ready, 1)
        for copy in leftward:
            copy.start()

    def send_first():
        send_right()
        for copy in rightward:
            copy.wait_send()

    pl.when(last)(send_first)
    get_state = [fetch(state.at[r], own.at[pl.ds(r * cols, cols)]) for r in range(rows)]
    get_vqkv = [fetch(w_vqkv.at[:, pl.ds(i * width, width)], vqkv.at[i]) for i in range(3)]
    pl.when(jnp.logical_not(last))(send_right)
    get_wet = fetch(wet_hbm, wet)
    get_vout = fetch(w_vout, vout)
    get_hqkv = [fetch(w_hqkv.at[:, pl.ds(i * width, width)], hqkv.at[i]) for i in range(3)]
    get_hout = fetch(w_hout, hout)

    for copy in get_state:
        copy.wait()
    tokens = own[...].reshape(count, width)
    values = tokens.astype(F32)
    factor = inverse_rms(values)
    joined = []
    for i in range(3):
        get_vqkv[i].wait()
        joined.append(dot(tokens, vqkv[i]))
        if i == 0:
            pl.when(me != 0)(send_left)
    row = lax.broadcasted_iota(jnp.int32, (count, count), 0)
    col = lax.broadcasted_iota(jnp.int32, (count, count), 1)
    query, keys = unit_heads(joined[0], factor), unit_heads(joined[1], factor)
    same_block = row // levels == col // levels
    context = contexts(weigh(query, keys, value_heads(joined[2], factor), same_block))
    get_vout.wait()
    tokens = (values + dot(context, vout[...])).astype(BF16)

    for copy in get_hqkv:
        copy.wait()
    get_wet.wait()
    key_block = lax.broadcasted_iota(jnp.int32, (1, count), 1) // levels
    wet_key = jnp.zeros((1, count), jnp.int32)
    for b in range(blocks):
        wet_key = jnp.where(key_block == b, wet[me * blocks + b], wet_key)
    near = jnp.abs(row // levels % cols - col // levels % cols) <= 1
    counted = jnp.logical_or(wet_key > 0, row // levels == key_block)
    own_mask = (row % levels == col % levels) & near & counted
    values = tokens.astype(F32)
    factor = inverse_rms(values)
    query = unit_heads(dot(tokens, hqkv[0]), factor)
    keys = unit_heads(dot(tokens, hqkv[1]), factor)
    value = value_heads(dot(tokens, hqkv[2]), factor)
    parts = weigh(query, keys, value, own_mask)

    def block_rows(array, first, number):
        return array[first * levels : (first + number) * levels]

    def inner_rows(array):
        return jnp.concatenate([block_rows(array, r * cols + 1, cols - 2) for r in range(rows)], axis=0)

    get_hout.wait()
    context = contexts([inner_rows(p) for p in parts])
    updated = (inner_rows(values) + dot(context, hout[...])).astype(BF16)
    updated = updated.reshape(rows, cols - 2, levels, width)
    for r in range(rows):
        out[pl.ds(r * cols + 1, cols - 2)] = updated[r]

    edges = [(side, r, r * cols + side * (cols - 1)) for side in range(2) for r in range(rows)]
    for side, r, b in edges:
        edge_base[side, r] = block_rows(values, b, 1)
    for h in range(HEADS):
        sums = jnp.concatenate([block_rows(parts[h], b, 1)[:, :head] for _, _, b in edges], axis=0)
        sums = dot(sums.astype(BF16), hout[pl.ds(h * head, head)])
        for e, (side, r, b) in enumerate(edges):
            edge_query[side, r, h] = block_rows(query[h], b, 1).astype(F32) * scale
            edge_total[side, r, h] = block_rows(parts[h], b, 1)[:, head:]
            edge_sum[side, r, h] = block_rows(sums, e, 1)

    def beside(step):
        side = jnp.where(me == 0, 1 - step, step)
        pl.when((step == 1) & (me == 0))(send_left)
        block = jnp.where(side == 0, left * blocks + cols - 1, right * blocks)
        first = wet[block] > 0
        pieces = []
        joined = [None] * 3
        for p in range(PARTS):
            arrived = pltpu.make_async_remote_copy(
                src_ref=halo.at[side, :, :, spans[p]],
                dst_ref=halo.at[side, :, :, spans[p]],
                send_sem=send_sems.at[side, p],
                recv_sem=recv_sems.at[side, p],
                device_id={"tile": left},
                device_id_type=MESH,
            )
            arrived.wait_recv()
            piece = jnp.where(first, halo[side, 0, :, spans[p]], halo[side, 1, :, spans[p]])
            pieces.append(piece)
            for i in range(3):
                product = dot(piece, vqkv[i, spans[p], :])
                joined[i] = product if p == 0 else joined[i] + product
        values = jnp.concatenate(pieces, axis=1).astype(F32)
        factor = inverse_rms(values)
        query, keys, value = [j * factor for j in joined]
        query_mean, key_mean = square_means(query), square_means(keys)
        value = value.astype(BF16)
        expon = []
        for h in range(HEADS):
            q, k = lanes(query, h), lanes(keys, h)
            scores = lax.dot_general(
                q.astype(BF16), k.astype(BF16), (((1,), (1,)), ((), ())), preferred_element_type=F32
            )
            by_key = jnp.broadcast_to(lax.rsqrt(key_mean[h] + EPSILON), (levels, head))
            by_key = jnp.transpose(by_key)[:levels]
            scores = scores * (lax.rsqrt(query_mean[h] + EPSILON) * scale) * by_key
            expon.append(jnp.exp(scores))
        mixed = values
        projected = [dot(lanes(value, h), vout[pl.ds(h * head, head)]).astype(BF16) for h in range(HEADS)]
        for h in range(HEADS):
            total = jnp.sum(expon[h], axis=-1, keepdims=True)
            mixed = mixed + dot(expon[h].astype(BF16), projected[h]) * (1.0 / total)
        tokens = mixed.astype(BF16)
        value = dot(tokens, hqkv[2]).astype(BF16)
        keys = dot(tokens, hqkv[1])
        factor = inverse_rms(mixed)
        projected = [dot(lanes(value, h), hout[pl.ds(h * head, head)]) for h in range(HEADS)]
        unit = [factor * lax.rsqrt(factor * factor * mean + EPSILON) for mean in square_means(keys)]
        for r in range(rows):
            updated = edge_base[side, r]
            for h in range(HEADS):
                scores = jnp.sum(edge_query[side, r, h] * lanes(keys, h), axis=-1, keepdims=True)
                expon = jnp.exp(scores * unit[h])
                inverse = 1.0 / (edge_total[side, r, h] + expon)
                inverse = jnp.concatenate([inverse] * HEADS, axis=1)
                updated = updated + (edge_sum[side, r, h] + (expon * factor) * projected[h]) * inverse
            out[r * cols + side * (cols - 1)] = updated.astype(BF16)

    loop(2, beside)

    def wait_right():
        for copy in rightward:
            copy.wait_send()

    pl.when(jnp.logical_not(last))(wait_right)
    for copy in leftward:
        copy.wait_send()


def on_device(tiles, state, wet, w_vqkv, w_vout, w_hqkv, w_hout):
    blocks, levels, width = state.shape
    rows = blocks // CB
    grid = state.reshape(rows, CB, levels, width)
    operands = (wet, grid, w_vqkv, w_vout, w_hqkv, w_hout)
    operands = [pltpu.with_memory_space_constraint(x, pltpu.HBM) for x in operands]
    any_space = pl.BlockSpec(memory_space=pl.ANY)
    small = blocks * levels <= ROWS
    if small:
        kernel, copies = small_kernel, (2, PARTS)
        scratch = [
            pltpu.VMEM((2, rows, levels, width), F32),
            pltpu.VMEM((2, rows, HEADS, levels, width // HEADS), F32),
            pltpu.VMEM((2, rows, HEADS, levels, width // HEADS), F32),
            pltpu.VMEM((2, rows, HEADS, levels, width), F32),
        ]
    else:
        kernel, copies = large_kernel, (2,)
        scratch = [pltpu.VMEM((blocks + 2, levels, width), BF16)]
    return pl.pallas_call(
        functools.partial(kernel, tiles),
        out_shape=jax.ShapeDtypeStruct((blocks, levels, width), BF16),
        in_specs=[any_space] * 6,
        out_specs=pl.BlockSpec(memory_space=pltpu.VMEM),
        scratch_shapes=[
            pltpu.SMEM(wet.shape, jnp.int32),
            pltpu.VMEM((blocks, levels, width), BF16),
            pltpu.VMEM((2, rows, levels, width), BF16),
            *scratch,
            pltpu.VMEM((3, width, width), BF16),
            pltpu.VMEM((width, width), BF16),
            pltpu.VMEM((3, width, width), BF16),
            pltpu.VMEM((width, width), BF16),
            pltpu.SemaphoreType.DMA((9 + rows,)),
            pltpu.SemaphoreType.REGULAR,
            pltpu.SemaphoreType.DMA(copies),
            pltpu.SemaphoreType.DMA(copies),
        ],
        compiler_params=pltpu.CompilerParams(
            collective_id=0, has_side_effects=True, vmem_limit_bytes=48 * 1024 * 1024
        ),
    )(*operands)


def solution(mesh):
    in_specs = (P(("grp", "tile"), None, None), P(), P(), P(), P(), P())
    out_specs = P(("grp", "tile"), None, None)
    return jax.shard_map(
        functools.partial(on_device, mesh.shape["tile"]),
        mesh=mesh,
        in_specs=in_specs,
        out_specs=out_specs,
        check_vma=False,
    )
```

```python
import functools
import math

import jax
import jax.numpy as jnp
from jax import lax
from jax.experimental import pallas as pl
from jax.experimental.pallas import tpu as pltpu
from jax.sharding import PartitionSpec as P

HEADS = 4
CB = 4
ROWS = 128
EPSILON = 1e-06
MESH = pl.DeviceIdType.MESH
BF16 = jnp.bfloat16
F32 = jnp.float32


def inverse_rms(values):
    return lax.rsqrt(jnp.mean(values * values, axis=-1, keepdims=True) + EPSILON)


def dot(a, b):
    return jnp.dot(a, b, preferred_element_type=F32)


def unit_heads(raw, factor):
    head = raw.shape[-1] // HEADS
    square = factor * factor
    out = []
    for h in range(HEADS):
        part = raw[:, h * head : (h + 1) * head]
        mean = jnp.mean(part * part, axis=-1, keepdims=True)
        out.append((part * (factor * lax.rsqrt(mean * square + EPSILON))).astype(BF16))
    return out


def value_heads(raw, factor):
    head = raw.shape[-1] // HEADS
    values = (raw * factor).astype(BF16)
    ones = jnp.ones((values.shape[0], head), BF16)
    return [
        jnp.concatenate([values[:, h * head : (h + 1) * head], ones], axis=1)
        for h in range(HEADS)
    ]


def weigh(query, keys, values, mask):
    parts = []
    for q, k, v in zip(query, keys, values):
        scale = 1.0 / math.sqrt(q.shape[-1])
        scores = lax.dot_general(q, k, (((1,), (1,)), ((), ())), preferred_element_type=F32)
        expon = jnp.where(mask, jnp.exp(scores * scale), 0.0).astype(BF16)
        parts.append(dot(expon, v))
    return parts


def contexts(parts):
    out = []
    for part in parts:
        head = part.shape[-1] // 2
        out.append((part[:, :head] / part[:, head:]).astype(BF16))
    return jnp.concatenate(out, axis=1)


def loop(count, body):
    if count == 1:
        body(0)
    else:
        lax.fori_loop(0, count, lambda i, c: (body(i), c)[1], 0)


def large_kernel(
    tiles,
    wet_hbm,
    state,
    w_vqkv,
    w_vout,
    w_hqkv,
    w_hout,
    out,
    wet,
    own,
    halo,
    mixed,
    vqkv,
    vout,
    hqkv,
    hout,
    sems,
    ready,
    send_sems,
    recv_sems,
):
    rows, cols, levels, width = state.shape
    blocks = rows * cols
    me = lax.axis_index("tile")
    right = lax.rem(me + 1, tiles)
    left = lax.rem(me + tiles - 1, tiles)

    barrier = pltpu.get_barrier_semaphore()
    pl.semaphore_signal(barrier, inc=1, device_id={"tile": left}, device_id_type=MESH)

    started = []

    def fetch(src, dst):
        copy = pltpu.make_async_copy(src, dst, sems.at[len(started)])
        copy.start()
        started.append(copy)
        return copy

    sends = [
        pltpu.make_async_remote_copy(
            src_ref=state.at[:, column],
            dst_ref=halo.at[i],
            send_sem=send_sems.at[i],
            recv_sem=recv_sems.at[i],
            device_id={"tile": side},
            device_id_type=MESH,
        )
        for i, (column, side) in enumerate(((cols - 1, right), (0, left)))
    ]

    def send_right():
        pl.semaphore_wait(barrier, 1)
        sends[0].start()
        pl.semaphore_signal(ready, inc=1, device_id={"tile": right}, device_id_type=MESH)

    def send_left():
        pl.semaphore_wait(ready, 1)
        sends[1].start()

    last = me == tiles - 1

    def send_first():
        send_right()
        sends[0].wait_send()

    pl.when(last)(send_first)
    get_state = [fetch(state.at[r], own.at[pl.ds(r * cols, cols)]) for r in range(rows)]
    get_vqkv = [fetch(w_vqkv.at[:, pl.ds(i * width, width)], vqkv.at[i]) for i in range(3)]
    pl.when(jnp.logical_not(last))(send_right)
    get_wet = fetch(wet_hbm, wet)
    get_vout = fetch(w_vout, vout)
    get_hqkv = [fetch(w_hqkv.at[:, pl.ds(i * width, width)], hqkv.at[i]) for i in range(3)]
    get_hout = fetch(w_hout, hout)

    def vertical(tokens):
        count = tokens.shape[0]
        values = tokens.astype(F32)
        factor = inverse_rms(values)
        joined = []
        for i in range(3):
            joined.append(dot(tokens, vqkv[i]))
        row = lax.broadcasted_iota(jnp.int32, (count, count), 0) // levels
        col = lax.broadcasted_iota(jnp.int32, (count, count), 1) // levels
        query, keys = unit_heads(joined[0], factor), unit_heads(joined[1], factor)
        context = contexts(weigh(query, keys, value_heads(joined[2], factor), row == col))
        return (values + dot(context, vout[...])).astype(BF16)

    group = max(1, min(blocks, ROWS // levels))
    for copy in get_state:
        copy.wait()
    pl.when(me != 0)(send_left)
    for copy in get_vqkv:
        copy.wait()
    get_vout.wait()

    def own_step(i):
        picked = pl.ds(i * group, group)
        tokens = own[picked].reshape(group * levels, width)
        mixed[picked] = vertical(tokens).reshape(group, levels, width)

    loop(blocks // group, own_step)

    pl.when(me == 0)(send_left)

    for copy in get_hqkv:
        copy.wait()
    get_wet.wait()

    step = min(levels, ROWS // blocks)
    n_own = blocks * step

    key_block = lax.broadcasted_iota(jnp.int32, (1, n_own), 1) // step
    wet_key = jnp.zeros((1, n_own), jnp.int32)
    for b in range(blocks):
        wet_key = jnp.where(key_block == b, wet[me * blocks + b], wet_key)
    row_id = lax.broadcasted_iota(jnp.int32, (n_own, n_own), 0)
    key_id = lax.broadcasted_iota(jnp.int32, (n_own, n_own), 1)
    near = jnp.abs(row_id // step % cols - key_id // step % cols) <= 1
    counted = jnp.logical_or(wet_key > 0, row_id // step == key_block)
    own_mask = (row_id % step == key_id % step) & near & counted

    edges = [r * cols + c for r in range(rows) for c in (0, cols - 1)]
    n_edge = len(edges) * step
    row_id = lax.broadcasted_iota(jnp.int32, (n_edge, 2 * step), 0)
    key_id = lax.broadcasted_iota(jnp.int32, (n_edge, 2 * step), 1)
    halo_mask = (row_id % step == key_id % step) & (row_id // step % 2 == key_id // step)

    def edge_rows(values):
        return jnp.concatenate([values[b * step : (b + 1) * step] for b in edges], axis=0)

    def inner_rows(values):
        spans = [((r * cols + 1) * step, (r * cols + cols - 1) * step) for r in range(rows)]
        return jnp.concatenate([values[first:end] for first, end in spans], axis=0)

    def among_own(i):
        picked = pl.ds(i * step, step)
        tokens = mixed[pl.ds(0, blocks), picked].reshape(n_own, width)
        values = tokens.astype(F32)
        factor = inverse_rms(values)
        query = unit_heads(dot(tokens, hqkv[0]), factor)
        keys = unit_heads(dot(tokens, hqkv[1]), factor)
        value = value_heads(dot(tokens, hqkv[2]), factor)
        parts = weigh(query, keys, value, own_mask)
        context = contexts([inner_rows(p) for p in parts])
        updated = (inner_rows(values) + dot(context, hout[...])).astype(BF16)
        updated = updated.reshape(rows, cols - 2, step, width)
        for r in range(rows):
            out[pl.ds(r * cols + 1, cols - 2), picked] = updated[r]
        query = [edge_rows(q) for q in query]
        return edge_rows(values), query, [edge_rows(p) for p in parts]

    def with_halo(i, beside, values, query, parts):
        picked = pl.ds(i * step, step)
        factor = inverse_rms(beside.astype(F32))
        keys = unit_heads(dot(beside, hqkv[1]), factor)
        value = value_heads(dot(beside, hqkv[2]), factor)
        more = weigh(query, keys, value, halo_mask)
        context = contexts([a + b for a, b in zip(parts, more)])
        updated = (values + dot(context, hout[...])).astype(BF16)
        for e, b in enumerate(edges):
            out[b, picked] = updated[e * step : (e + 1) * step]

    get_hout.wait()
    for i, copy in enumerate(sends):
        copy.wait_recv()
        block = (left * blocks + cols - 1, right * blocks)[i]
        picked_halo = jnp.where(wet[block] > 0, halo[i, 0], halo[i, 1])
        mixed[blocks + i] = vertical(picked_halo)

    def level_step(i):
        beside = mixed[pl.ds(blocks, 2), pl.ds(i * step, step)]
        with_halo(i, beside.reshape(2 * step, width), *among_own(i))

    loop(levels // step, level_step)
    pl.when(jnp.logical_not(last))(sends[0].wait_send)
    sends[1].wait_send()


def lanes(values, h):
    head = values.shape[-1] // HEADS
    return values[..., h * head : (h + 1) * head]


def square_means(values):
    return [jnp.mean(lanes(values, h) * lanes(values, h), axis=-1, keepdims=True) for h in range(HEADS)]


def small_kernel(
    tiles,
    wet_hbm,
    state,
    w_vqkv,
    w_vout,
    w_hqkv,
    w_hout,
    out,
    wet,
    own,
    halo,
    edge_base,
    edge_query,
    edge_total,
    edge_sum,
    joint,
    vout,
    hqkv,
    hout,
    folded,
    sems,
    ready,
    send_sems,
    recv_sems,
):
    rows, cols, levels, width = state.shape
    blocks = rows * cols
    head = width // HEADS
    count = blocks * levels
    scale = 1.0 / math.sqrt(head)
    me = lax.axis_index("tile")
    right = lax.rem(me + 1, tiles)
    left = lax.rem(me + tiles - 1, tiles)
    last = me == tiles - 1

    barrier = pltpu.get_barrier_semaphore()
    pl.semaphore_signal(barrier, inc=1, device_id={"tile": left}, device_id_type=MESH)

    started = []

    def fetch(src, dst):
        copy = pltpu.make_async_copy(src, dst, sems.at[len(started)])
        copy.start()
        started.append(copy)
        return copy

    def halo_copy(i, column, side):
        return pltpu.make_async_remote_copy(
            src_ref=state.at[:, column],
            dst_ref=halo.at[i],
            send_sem=send_sems.at[i],
            recv_sem=recv_sems.at[i],
            device_id={"tile": side},
            device_id_type=MESH,
        )

    rightward = halo_copy(0, cols - 1, right)
    leftward = halo_copy(1, 0, left)

    def send_right():
        pl.semaphore_wait(barrier, 1)
        rightward.start()
        pl.semaphore_signal(ready, inc=1, device_id={"tile": right}, device_id_type=MESH)

    def send_left():
        pl.semaphore_wait(ready, 1)
        leftward.start()

    def send_first():
        send_right()
        rightward.wait_send()

    pl.when(last)(send_first)
    get_state = [fetch(state.at[r], own.at[pl.ds(r * cols, cols)]) for r in range(rows)]
    third = [pl.ds(i * width, width) for i in range(4)]
    get_vqkv = [fetch(w_vqkv.at[:, third[i]], joint.at[:, third[i]]) for i in range(3)]
    pl.when(jnp.logical_not(last))(send_right)
    get_wet = fetch(wet_hbm, wet)
    get_vout = fetch(w_vout, vout)
    get_hqkv = [fetch(w_hqkv.at[:, third[i]], hqkv.at[:, third[i]]) for i in range(2)]
    get_hqkv.append(fetch(w_hqkv.at[:, third[2]], joint.at[:, third[3]]))
    get_hout = fetch(w_hout, hout)

    for copy in get_state:
        copy.wait()
    tokens = own[...].reshape(count, width)
    values = tokens.astype(F32)
    factor = inverse_rms(values)
    joined = []
    for i in range(3):
        get_vqkv[i].wait()
        joined.append(dot(tokens, joint[:, third[i]]))
        if i == 0:
            pl.when(me != 0)(send_left)
    row = lax.broadcasted_iota(jnp.int32, (count, count), 0)
    col = lax.broadcasted_iota(jnp.int32, (count, count), 1)
    query, keys = unit_heads(joined[0], factor), unit_heads(joined[1], factor)
    same_block = row // levels == col // levels
    context = contexts(weigh(query, keys, value_heads(joined[2], factor), same_block))
    get_vout.wait()
    tokens = (values + dot(context, vout[...])).astype(BF16)

    for copy in get_hqkv:
        copy.wait()
    get_wet.wait()
    key_block = lax.broadcasted_iota(jnp.int32, (1, count), 1) // levels
    wet_key = jnp.zeros((1, count), jnp.int32)
    for b in range(blocks):
        wet_key = jnp.where(key_block == b, wet[me * blocks + b], wet_key)
    near = jnp.abs(row // levels % cols - col // levels % cols) <= 1
    counted = jnp.logical_or(wet_key > 0, row // levels == key_block)
    own_mask = (row % levels == col % levels) & near & counted
    values = tokens.astype(F32)
    factor = inverse_rms(values)
    query = unit_heads(dot(tokens, hqkv[:, third[0]]), factor)
    keys = unit_heads(dot(tokens, hqkv[:, third[1]]), factor)
    value = value_heads(dot(tokens, joint[:, third[3]]), factor)
    parts = weigh(query, keys, value, own_mask)

    def block_rows(array, first, number):
        return array[first * levels : (first + number) * levels]

    def inner_rows(array):
        return jnp.concatenate([block_rows(array, r * cols + 1, cols - 2) for r in range(rows)], axis=0)

    get_hout.wait()
    context = contexts([inner_rows(p) for p in parts])
    updated = (inner_rows(values) + dot(context, hout[...])).astype(BF16)
    updated = updated.reshape(rows, cols - 2, levels, width)
    for r in range(rows):
        out[pl.ds(r * cols + 1, cols - 2)] = updated[r]

    edges = [(side, r, r * cols + side * (cols - 1)) for side in range(2) for r in range(rows)]
    for side, r, b in edges:
        edge_base[side, r] = block_rows(values, b, 1)
    for h in range(HEADS):
        sums = jnp.concatenate([block_rows(parts[h], b, 1)[:, :head] for _, _, b in edges], axis=0)
        sums = dot(sums.astype(BF16), hout[pl.ds(h * head, head)])
        for e, (side, r, b) in enumerate(edges):
            edge_query[side, r, h] = block_rows(query[h], b, 1).astype(F32) * scale
            edge_total[side, r, h] = block_rows(parts[h], b, 1)[:, head:]
            edge_sum[side, r, h] = block_rows(sums, e, 1)

    folded[...] = dot(vout[...], joint[:, third[3]]).astype(BF16)

    def beside(step):
        side = jnp.where(me == 0, 1 - step, step)
        block = jnp.where(side == 0, left * blocks + cols - 1, right * blocks)
        first = wet[block] > 0
        arrived = pltpu.make_async_remote_copy(
            src_ref=halo.at[side],
            dst_ref=halo.at[side],
            send_sem=send_sems.at[side],
            recv_sem=recv_sems.at[side],
            device_id={"tile": left},
            device_id_type=MESH,
        )
        arrived.wait_recv()
        tokens = jnp.where(first, halo[side, 0], halo[side, 1])
        joined = dot(tokens, joint[...])
        joined = [joined[:, i * width : (i + 1) * width] for i in range(4)]
        values = tokens.astype(F32)
        factor = inverse_rms(values)
        query, keys, value = [j * factor for j in joined[:3]]
        next_value = joined[3]
        query_mean, key_mean = square_means(query), square_means(keys)
        value = value.astype(BF16)
        expon = []
        for h in range(HEADS):
            q, k = lanes(query, h), lanes(keys, h)
            scores = lax.dot_general(
                q.astype(BF16), k.astype(BF16), (((1,), (1,)), ((), ())), preferred_element_type=F32
            )
            by_key = jnp.broadcast_to(lax.rsqrt(key_mean[h] + EPSILON), (levels, head))
            by_key = jnp.transpose(by_key)[:levels]
            scores = scores * (lax.rsqrt(query_mean[h] + EPSILON) * scale) * by_key
            expon.append(jnp.exp(scores))
        mixed = values
        value = [lanes(value, h) for h in range(HEADS)]
        rows_of = [pl.ds(h * head, head) for h in range(HEADS)]
        projected = [dot(value[h], vout[rows_of[h]]).astype(BF16) for h in range(HEADS)]
        twice = [dot(value[h], folded[rows_of[h]]).astype(BF16) for h in range(HEADS)]
        inverse = [1.0 / jnp.sum(e, axis=-1, keepdims=True) for e in expon]
        expon = [e.astype(BF16) for e in expon]
        for h in range(HEADS):
            mixed = mixed + dot(expon[h], projected[h]) * inverse[h]
        for h in range(HEADS):
            next_value = next_value + dot(expon[h], twice[h]) * inverse[h]
        value = next_value.astype(BF16)
        keys = dot(mixed.astype(BF16), hqkv[:, third[1]])
        factor = inverse_rms(mixed)
        projected = [dot(lanes(value, h), hout[rows_of[h]]) for h in range(HEADS)]
        unit = [factor * lax.rsqrt(factor * factor * mean + EPSILON) for mean in square_means(keys)]
        for r in range(rows):
            updated = edge_base[side, r]
            for h in range(HEADS):
                scores = jnp.sum(edge_query[side, r, h] * lanes(keys, h), axis=-1, keepdims=True)
                expon = jnp.exp(scores * unit[h])
                inverse = 1.0 / (edge_total[side, r, h] + expon)
                inverse = jnp.concatenate([inverse] * HEADS, axis=1)
                updated = updated + (edge_sum[side, r, h] + (expon * factor) * projected[h]) * inverse
            out[r * cols + side * (cols - 1)] = updated.astype(BF16)

    pl.when(me == 0)(send_left)
    loop(2, beside)

    pl.when(jnp.logical_not(last))(rightward.wait_send)
    leftward.wait_send()


def on_device(tiles, state, wet, w_vqkv, w_vout, w_hqkv, w_hout):
    blocks, levels, width = state.shape
    rows = blocks // CB
    grid = state.reshape(rows, CB, levels, width)
    operands = (wet, grid, w_vqkv, w_vout, w_hqkv, w_hout)
    operands = [pltpu.with_memory_space_constraint(x, pltpu.HBM) for x in operands]
    any_space = pl.BlockSpec(memory_space=pl.ANY)
    head = width // HEADS
    whole = pltpu.VMEM((width, width), BF16)
    if blocks * levels <= ROWS:
        kernel = small_kernel
        scratch = [
            pltpu.VMEM((2, rows, levels, width), F32),
            pltpu.VMEM((2, rows, HEADS, levels, head), F32),
            pltpu.VMEM((2, rows, HEADS, levels, head), F32),
            pltpu.VMEM((2, rows, HEADS, levels, width), F32),
            pltpu.VMEM((width, 4 * width), BF16),
            whole,
            pltpu.VMEM((width, 2 * width), BF16),
            whole,
            whole,
        ]
    else:
        kernel = large_kernel
        three = pltpu.VMEM((3, width, width), BF16)
        scratch = [pltpu.VMEM((blocks + 2, levels, width), BF16), three, whole, three, whole]
    return pl.pallas_call(
        functools.partial(kernel, tiles),
        out_shape=jax.ShapeDtypeStruct((blocks, levels, width), BF16),
        in_specs=[any_space] * 6,
        out_specs=pl.BlockSpec(memory_space=pltpu.VMEM),
        scratch_shapes=[
            pltpu.SMEM(wet.shape, jnp.int32),
            pltpu.VMEM((blocks, levels, width), BF16),
            pltpu.VMEM((2, rows, levels, width), BF16),
            *scratch,
            pltpu.SemaphoreType.DMA((9 + rows,)),
            pltpu.SemaphoreType.REGULAR,
            pltpu.SemaphoreType.DMA((2,)),
            pltpu.SemaphoreType.DMA((2,)),
        ],
        compiler_params=pltpu.CompilerParams(
            collective_id=0, has_side_effects=True, vmem_limit_bytes=48 * 1024 * 1024
        ),
    )(*operands)


def solution(mesh):
    in_specs = (P(("grp", "tile"), None, None), P(), P(), P(), P(), P())
    out_specs = P(("grp", "tile"), None, None)
    return jax.shard_map(
        functools.partial(on_device, mesh.shape["tile"]),
        mesh=mesh,
        in_specs=in_specs,
        out_specs=out_specs,
        check_vma=False,
    )
```

```python
import functools
import math

import jax
import jax.numpy as jnp
from jax import lax
from jax.experimental import pallas as pl
from jax.experimental.pallas import tpu as pltpu
from jax.sharding import PartitionSpec as P

HEADS = 4
CB = 4
ROWS = 128
PIECES = 4
EPSILON = 1e-06
MESH = pl.DeviceIdType.MESH
BF16 = jnp.bfloat16
F32 = jnp.float32


def inverse_rms(values):
    return lax.rsqrt(jnp.mean(values * values, axis=-1, keepdims=True) + EPSILON)


def dot(a, b):
    return jnp.dot(a, b, preferred_element_type=F32)


def unit_heads(raw, factor):
    head = raw.shape[-1] // HEADS
    square = factor * factor
    out = []
    for h in range(HEADS):
        part = raw[:, h * head : (h + 1) * head]
        mean = jnp.mean(part * part, axis=-1, keepdims=True)
        out.append((part * (factor * lax.rsqrt(mean * square + EPSILON))).astype(BF16))
    return out


def value_heads(raw, factor):
    head = raw.shape[-1] // HEADS
    values = (raw * factor).astype(BF16)
    ones = jnp.ones((values.shape[0], head), BF16)
    return [
        jnp.concatenate([values[:, h * head : (h + 1) * head], ones], axis=1)
        for h in range(HEADS)
    ]


def weigh(query, keys, values, mask):
    parts = []
    for q, k, v in zip(query, keys, values):
        scale = 1.0 / math.sqrt(q.shape[-1])
        scores = lax.dot_general(q, k, (((1,), (1,)), ((), ())), preferred_element_type=F32)
        expon = jnp.where(mask, jnp.exp(scores * scale), 0.0).astype(BF16)
        parts.append(dot(expon, v))
    return parts


def contexts(parts):
    out = []
    for part in parts:
        head = part.shape[-1] // 2
        out.append((part[:, :head] / part[:, head:]).astype(BF16))
    return jnp.concatenate(out, axis=1)


def loop(count, body):
    if count == 1:
        body(0)
    else:
        lax.fori_loop(0, count, lambda i, c: (body(i), c)[1], 0)


def large_kernel(
    tiles,
    wet_hbm,
    state,
    w_vqkv,
    w_vout,
    w_hqkv,
    w_hout,
    out,
    wet,
    own,
    halo,
    mixed,
    vqkv,
    vout,
    hqkv,
    hout,
    sems,
    ready,
    send_sems,
    recv_sems,
):
    rows, cols, levels, width = state.shape
    blocks = rows * cols
    me = lax.axis_index("tile")
    right = lax.rem(me + 1, tiles)
    left = lax.rem(me + tiles - 1, tiles)

    barrier = pltpu.get_barrier_semaphore()
    pl.semaphore_signal(barrier, inc=1, device_id={"tile": left}, device_id_type=MESH)

    started = []

    def fetch(src, dst):
        copy = pltpu.make_async_copy(src, dst, sems.at[len(started)])
        copy.start()
        started.append(copy)
        return copy

    sends = [
        pltpu.make_async_remote_copy(
            src_ref=state.at[:, column],
            dst_ref=halo.at[i],
            send_sem=send_sems.at[i],
            recv_sem=recv_sems.at[i],
            device_id={"tile": side},
            device_id_type=MESH,
        )
        for i, (column, side) in enumerate(((cols - 1, right), (0, left)))
    ]

    def send_right():
        pl.semaphore_wait(barrier, 1)
        sends[0].start()
        pl.semaphore_signal(ready, inc=1, device_id={"tile": right}, device_id_type=MESH)

    def send_left():
        pl.semaphore_wait(ready, 1)
        sends[1].start()

    last = me == tiles - 1

    def send_first():
        send_right()
        sends[0].wait_send()

    pl.when(last)(send_first)
    get_state = [fetch(state.at[r], own.at[pl.ds(r * cols, cols)]) for r in range(rows)]
    get_vqkv = [fetch(w_vqkv.at[:, pl.ds(i * width, width)], vqkv.at[i]) for i in range(3)]
    pl.when(jnp.logical_not(last))(send_right)
    get_wet = fetch(wet_hbm, wet)
    get_vout = fetch(w_vout, vout)
    get_hqkv = [fetch(w_hqkv.at[:, pl.ds(i * width, width)], hqkv.at[i]) for i in range(3)]
    get_hout = fetch(w_hout, hout)

    def vertical(tokens):
        count = tokens.shape[0]
        values = tokens.astype(F32)
        factor = inverse_rms(values)
        joined = []
        for i in range(3):
            joined.append(dot(tokens, vqkv[i]))
        row = lax.broadcasted_iota(jnp.int32, (count, count), 0) // levels
        col = lax.broadcasted_iota(jnp.int32, (count, count), 1) // levels
        query, keys = unit_heads(joined[0], factor), unit_heads(joined[1], factor)
        context = contexts(weigh(query, keys, value_heads(joined[2], factor), row == col))
        return (values + dot(context, vout[...])).astype(BF16)

    group = max(1, min(blocks, ROWS // levels))
    for copy in get_state:
        copy.wait()
    pl.when(me != 0)(send_left)
    for copy in get_vqkv:
        copy.wait()
    get_vout.wait()

    def own_step(i):
        picked = pl.ds(i * group, group)
        tokens = own[picked].reshape(group * levels, width)
        mixed[picked] = vertical(tokens).reshape(group, levels, width)

    loop(blocks // group, own_step)

    pl.when(me == 0)(send_left)

    for copy in get_hqkv:
        copy.wait()
    get_wet.wait()

    step = min(levels, ROWS // blocks)
    n_own = blocks * step

    key_block = lax.broadcasted_iota(jnp.int32, (1, n_own), 1) // step
    wet_key = jnp.zeros((1, n_own), jnp.int32)
    for b in range(blocks):
        wet_key = jnp.where(key_block == b, wet[me * blocks + b], wet_key)
    row_id = lax.broadcasted_iota(jnp.int32, (n_own, n_own), 0)
    key_id = lax.broadcasted_iota(jnp.int32, (n_own, n_own), 1)
    near = jnp.abs(row_id // step % cols - key_id // step % cols) <= 1
    counted = jnp.logical_or(wet_key > 0, row_id // step == key_block)
    own_mask = (row_id % step == key_id % step) & near & counted

    edges = [r * cols + c for r in range(rows) for c in (0, cols - 1)]
    n_edge = len(edges) * step
    row_id = lax.broadcasted_iota(jnp.int32, (n_edge, 2 * step), 0)
    key_id = lax.broadcasted_iota(jnp.int32, (n_edge, 2 * step), 1)
    halo_mask = (row_id % step == key_id % step) & (row_id // step % 2 == key_id // step)

    def edge_rows(values):
        return jnp.concatenate([values[b * step : (b + 1) * step] for b in edges], axis=0)

    def inner_rows(values):
        spans = [((r * cols + 1) * step, (r * cols + cols - 1) * step) for r in range(rows)]
        return jnp.concatenate([values[first:end] for first, end in spans], axis=0)

    def among_own(i):
        picked = pl.ds(i * step, step)
        tokens = mixed[pl.ds(0, blocks), picked].reshape(n_own, width)
        values = tokens.astype(F32)
        factor = inverse_rms(values)
        query = unit_heads(dot(tokens, hqkv[0]), factor)
        keys = unit_heads(dot(tokens, hqkv[1]), factor)
        value = value_heads(dot(tokens, hqkv[2]), factor)
        parts = weigh(query, keys, value, own_mask)
        context = contexts([inner_rows(p) for p in parts])
        updated = (inner_rows(values) + dot(context, hout[...])).astype(BF16)
        updated = updated.reshape(rows, cols - 2, step, width)
        for r in range(rows):
            out[pl.ds(r * cols + 1, cols - 2), picked] = updated[r]
        query = [edge_rows(q) for q in query]
        return edge_rows(values), query, [edge_rows(p) for p in parts]

    def with_halo(i, beside, values, query, parts):
        picked = pl.ds(i * step, step)
        factor = inverse_rms(beside.astype(F32))
        keys = unit_heads(dot(beside, hqkv[1]), factor)
        value = value_heads(dot(beside, hqkv[2]), factor)
        more = weigh(query, keys, value, halo_mask)
        context = contexts([a + b for a, b in zip(parts, more)])
        updated = (values + dot(context, hout[...])).astype(BF16)
        for e, b in enumerate(edges):
            out[b, picked] = updated[e * step : (e + 1) * step]

    get_hout.wait()
    for i, copy in enumerate(sends):
        copy.wait_recv()
        block = (left * blocks + cols - 1, right * blocks)[i]
        picked_halo = jnp.where(wet[block] > 0, halo[i, 0], halo[i, 1])
        mixed[blocks + i] = vertical(picked_halo)

    def level_step(i):
        beside = mixed[pl.ds(blocks, 2), pl.ds(i * step, step)]
        with_halo(i, beside.reshape(2 * step, width), *among_own(i))

    loop(levels // step, level_step)
    pl.when(jnp.logical_not(last))(sends[0].wait_send)
    sends[1].wait_send()


def lanes(values, h):
    head = values.shape[-1] // HEADS
    return values[..., h * head : (h + 1) * head]


def square_means(values):
    return [jnp.mean(lanes(values, h) * lanes(values, h), axis=-1, keepdims=True) for h in range(HEADS)]


def small_kernel(
    tiles,
    wet_hbm,
    state,
    w_vqkv,
    w_vout,
    w_hqkv,
    w_hout,
    out,
    wet,
    own,
    halo,
    edge_base,
    edge_query,
    edge_total,
    edge_sum,
    joint,
    vout,
    hqkv,
    hout,
    folded,
    ready,
    send_sems,
    recv_sems,
):
    rows, cols, levels, width = state.shape
    blocks = rows * cols
    head = width // HEADS
    count = blocks * levels
    scale = 1.0 / math.sqrt(head)
    me = lax.axis_index("tile")
    right = lax.rem(me + 1, tiles)
    left = lax.rem(me + tiles - 1, tiles)
    last = me == tiles - 1

    barrier = pltpu.get_barrier_semaphore()
    pl.semaphore_signal(barrier, inc=1, device_id={"tile": left}, device_id_type=MESH)

    third = [pl.ds(i * width, width) for i in range(4)]
    spans = [pl.ds(p * width // PIECES, width // PIECES) for p in range(PIECES)]

    def halo_copy(i, span, sem, column, side):
        return pltpu.make_async_remote_copy(
            src_ref=state.at[:, column, :, span],
            dst_ref=halo.at[i, :, :, span],
            send_sem=send_sems.at[i],
            recv_sem=recv_sems.at[sem],
            device_id={"tile": side},
            device_id_type=MESH,
        )

    full = pl.ds(0, width)
    rightward = [halo_copy(0, span, p, cols - 1, right) for p, span in enumerate(spans)]
    leftward = halo_copy(1, full, len(spans), 0, left)

    def wait_sent(i):
        halo_copy(i, full, 0, 0, right).wait_send()

    def send_right():
        pl.semaphore_wait(barrier, 1)
        for copy in rightward:
            copy.start()
        pl.semaphore_signal(ready, inc=1, device_id={"tile": right}, device_id_type=MESH)

    def send_left():
        pl.semaphore_wait(ready, 1)
        leftward.start()

    def send_first():
        send_right()
        wait_sent(0)

    def own_blocks(sems):
        started = []

        def fetch(src, dst):
            copy = pltpu.make_async_copy(src, dst, sems.at[len(started)])
            copy.start()
            started.append(copy)
            return copy

        pl.when(last)(send_first)
        get_state = [fetch(state.at[r], own.at[pl.ds(r * cols, cols)]) for r in range(rows)]
        get_vqkv = [fetch(w_vqkv.at[:, third[i]], joint.at[:, third[i]]) for i in range(3)]
        pl.when(jnp.logical_not(last))(send_right)
        get_wet = fetch(wet_hbm, wet)
        get_vout = fetch(w_vout, vout)
        get_hqkv = [fetch(w_hqkv.at[:, third[i]], hqkv.at[:, third[i]]) for i in range(2)]
        get_hqkv.append(fetch(w_hqkv.at[:, third[2]], joint.at[:, third[3]]))
        get_hout = fetch(w_hout, hout)

        for copy in get_state:
            copy.wait()
        tokens = own[...].reshape(count, width)
        values = tokens.astype(F32)
        factor = inverse_rms(values)
        joined = []
        for i in range(3):
            get_vqkv[i].wait()
            joined.append(dot(tokens, joint[:, third[i]]))
            if i == 0:
                pl.when(me != 0)(send_left)
        row = lax.broadcasted_iota(jnp.int32, (count, count), 0)
        col = lax.broadcasted_iota(jnp.int32, (count, count), 1)
        query, keys = unit_heads(joined[0], factor), unit_heads(joined[1], factor)
        same_block = row // levels == col // levels
        context = contexts(weigh(query, keys, value_heads(joined[2], factor), same_block))
        get_vout.wait()
        tokens = (values + dot(context, vout[...])).astype(BF16)

        for copy in get_hqkv:
            copy.wait()
        get_wet.wait()
        key_block = lax.broadcasted_iota(jnp.int32, (1, count), 1) // levels
        wet_key = jnp.zeros((1, count), jnp.int32)
        for b in range(blocks):
            wet_key = jnp.where(key_block == b, wet[me * blocks + b], wet_key)
        near = jnp.abs(row // levels % cols - col // levels % cols) <= 1
        counted = jnp.logical_or(wet_key > 0, row // levels == key_block)
        own_mask = (row % levels == col % levels) & near & counted
        values = tokens.astype(F32)
        factor = inverse_rms(values)
        query = unit_heads(dot(tokens, hqkv[:, third[0]]), factor)
        keys = unit_heads(dot(tokens, hqkv[:, third[1]]), factor)
        value = value_heads(dot(tokens, joint[:, third[3]]), factor)
        parts = weigh(query, keys, value, own_mask)

        def block_rows(array, first, number):
            return array[first * levels : (first + number) * levels]

        def inner_rows(array):
            return jnp.concatenate([block_rows(array, r * cols + 1, cols - 2) for r in range(rows)], axis=0)

        get_hout.wait()
        context = contexts([inner_rows(p) for p in parts])
        updated = (inner_rows(values) + dot(context, hout[...])).astype(BF16)
        updated = updated.reshape(rows, cols - 2, levels, width)
        for r in range(rows):
            out[pl.ds(r * cols + 1, cols - 2)] = updated[r]

        edges = [(side, r, r * cols + side * (cols - 1)) for side in range(2) for r in range(rows)]
        for side, r, b in edges:
            edge_base[side, r] = block_rows(values, b, 1)
        for h in range(HEADS):
            sums = jnp.concatenate([block_rows(parts[h], b, 1)[:, :head] for _, _, b in edges], axis=0)
            sums = dot(sums.astype(BF16), hout[pl.ds(h * head, head)])
            for e, (side, r, b) in enumerate(edges):
                edge_query[side, r, h] = block_rows(query[h], b, 1).astype(F32) * scale
                edge_total[side, r, h] = block_rows(parts[h], b, 1)[:, head:]
                edge_sum[side, r, h] = block_rows(sums, e, 1)

        folded[...] = dot(vout[...], joint[:, third[3]]).astype(BF16)

    def beside(step):
        side = jnp.where(me == 0, 1 - step, step)
        block = jnp.where(side == 0, left * blocks + cols - 1, right * blocks)
        first = wet[block] > 0
        pieces = []
        pl.when(side == 1)(leftward.wait_recv)
        for p, span in enumerate(spans):
            pl.when(side == 0)(rightward[p].wait_recv)
            pieces.append(jnp.where(first, halo[side, 0, :, span], halo[side, 1, :, span]))
            product = dot(pieces[p], joint[span, pl.ds(0, 3 * width)])
            joined = product if p == 0 else joined + product
        tokens = jnp.concatenate(pieces, axis=1)
        joined = [joined[:, i * width : (i + 1) * width] for i in range(3)]
        next_value = dot(tokens, joint[:, pl.ds(3 * width, width)])
        values = tokens.astype(F32)
        factor = inverse_rms(values)
        query, keys, value = [j * factor for j in joined[:3]]
        query_mean, key_mean = square_means(query), square_means(keys)
        value = value.astype(BF16)
        expon = []
        for h in range(HEADS):
            q, k = lanes(query, h), lanes(keys, h)
            scores = lax.dot_general(
                q.astype(BF16), k.astype(BF16), (((1,), (1,)), ((), ())), preferred_element_type=F32
            )
            by_key = jnp.broadcast_to(lax.rsqrt(key_mean[h] + EPSILON), (levels, head))
            by_key = jnp.transpose(by_key)[:levels]
            scores = scores * (lax.rsqrt(query_mean[h] + EPSILON) * scale) * by_key
            expon.append(jnp.exp(scores))
        mixed = values
        value = [lanes(value, h) for h in range(HEADS)]
        rows_of = [pl.ds(h * head, head) for h in range(HEADS)]
        projected = [dot(value[h], vout[rows_of[h]]).astype(BF16) for h in range(HEADS)]
        twice = [dot(value[h], folded[rows_of[h]]).astype(BF16) for h in range(HEADS)]
        inverse = [1.0 / jnp.sum(e, axis=-1, keepdims=True) for e in expon]
        expon = [e.astype(BF16) for e in expon]
        for h in range(HEADS):
            mixed = mixed + dot(expon[h], projected[h]) * inverse[h]
        for h in range(HEADS):
            next_value = next_value + dot(expon[h], twice[h]) * inverse[h]
        value = next_value.astype(BF16)
        keys = dot(mixed.astype(BF16), hqkv[:, third[1]])
        factor = inverse_rms(mixed)
        projected = [dot(lanes(value, h), hout[rows_of[h]]) for h in range(HEADS)]
        unit = [factor * lax.rsqrt(factor * factor * mean + EPSILON) for mean in square_means(keys)]
        for r in range(rows):
            updated = edge_base[side, r]
            for h in range(HEADS):
                scores = jnp.sum(edge_query[side, r, h] * lanes(keys, h), axis=-1, keepdims=True)
                expon = jnp.exp(scores * unit[h])
                inverse = 1.0 / (edge_total[side, r, h] + expon)
                inverse = jnp.concatenate([inverse] * HEADS, axis=1)
                updated = updated + (edge_sum[side, r, h] + (expon * factor) * projected[h]) * inverse
            out[r * cols + side * (cols - 1)] = updated.astype(BF16)

    pl.run_scoped(own_blocks, pltpu.SemaphoreType.DMA((9 + rows,)))
    pl.when(me == 0)(send_left)
    loop(2, beside)

    pl.when(jnp.logical_not(last))(functools.partial(wait_sent, 0))
    wait_sent(1)


def on_device(tiles, state, wet, w_vqkv, w_vout, w_hqkv, w_hout):
    blocks, levels, width = state.shape
    rows = blocks // CB
    grid = state.reshape(rows, CB, levels, width)
    operands = (wet, grid, w_vqkv, w_vout, w_hqkv, w_hout)
    operands = [pltpu.with_memory_space_constraint(x, pltpu.HBM) for x in operands]
    any_space = pl.BlockSpec(memory_space=pl.ANY)
    head = width // HEADS
    two = pltpu.SemaphoreType.DMA((2,))
    whole = pltpu.VMEM((width, width), BF16)
    if blocks * levels <= ROWS:
        kernel = small_kernel
        semaphores = [pltpu.SemaphoreType.REGULAR, two, pltpu.SemaphoreType.DMA((PIECES + 1,))]
        scratch = [
            pltpu.VMEM((2, rows, levels, width), F32),
            pltpu.VMEM((2, rows, HEADS, levels, head), F32),
            pltpu.VMEM((2, rows, HEADS, levels, head), F32),
            pltpu.VMEM((2, rows, HEADS, levels, width), F32),
            pltpu.VMEM((width, 4 * width), BF16),
            whole,
            pltpu.VMEM((width, 2 * width), BF16),
            whole,
            whole,
        ]
    else:
        kernel = large_kernel
        semaphores = [pltpu.SemaphoreType.DMA((9 + rows,)), pltpu.SemaphoreType.REGULAR, two, two]
        three = pltpu.VMEM((3, width, width), BF16)
        scratch = [pltpu.VMEM((blocks + 2, levels, width), BF16), three, whole, three, whole]
    return pl.pallas_call(
        functools.partial(kernel, tiles),
        out_shape=jax.ShapeDtypeStruct((blocks, levels, width), BF16),
        in_specs=[any_space] * 6,
        out_specs=pl.BlockSpec(memory_space=pltpu.VMEM),
        scratch_shapes=[
            pltpu.SMEM(wet.shape, jnp.int32),
            pltpu.VMEM((blocks, levels, width), BF16),
            pltpu.VMEM((2, rows, levels, width), BF16),
            *scratch,
            *semaphores,
        ],
        compiler_params=pltpu.CompilerParams(
            collective_id=0, has_side_effects=True, vmem_limit_bytes=48 * 1024 * 1024
        ),
    )(*operands)


def solution(mesh):
    in_specs = (P(("grp", "tile"), None, None), P(), P(), P(), P(), P())
    out_specs = P(("grp", "tile"), None, None)
    return jax.shard_map(
        functools.partial(on_device, mesh.shape["tile"]),
        mesh=mesh,
        in_specs=in_specs,
        out_specs=out_specs,
        check_vma=False,
    )
```

```python
import functools
import math

import jax
import jax.numpy as jnp
from jax import lax
from jax.experimental import pallas as pl
from jax.experimental.pallas import tpu as pltpu
from jax.sharding import PartitionSpec as P

HEADS = 4
CB = 4
ROWS = 128
PIECES = 4
EPSILON = 1e-06
MESH = pl.DeviceIdType.MESH
BF16 = jnp.bfloat16
F32 = jnp.float32


def inverse_rms(values):
    return lax.rsqrt(jnp.mean(values * values, axis=-1, keepdims=True) + EPSILON)


def dot(a, b):
    return jnp.dot(a, b, preferred_element_type=F32)


def unit_heads(raw, factor):
    head = raw.shape[-1] // HEADS
    square = factor * factor
    out = []
    for h in range(HEADS):
        part = raw[:, h * head : (h + 1) * head]
        mean = jnp.mean(part * part, axis=-1, keepdims=True)
        out.append((part * (factor * lax.rsqrt(mean * square + EPSILON))).astype(BF16))
    return out


def value_heads(raw, factor):
    head = raw.shape[-1] // HEADS
    values = (raw * factor).astype(BF16)
    ones = jnp.ones((values.shape[0], head), BF16)
    return [
        jnp.concatenate([values[:, h * head : (h + 1) * head], ones], axis=1)
        for h in range(HEADS)
    ]


def weigh(query, keys, values, mask):
    parts = []
    for q, k, v in zip(query, keys, values):
        scale = 1.0 / math.sqrt(q.shape[-1])
        scores = lax.dot_general(q, k, (((1,), (1,)), ((), ())), preferred_element_type=F32)
        expon = jnp.where(mask, jnp.exp(scores * scale), 0.0).astype(BF16)
        parts.append(dot(expon, v))
    return parts


def contexts(parts):
    out = []
    for part in parts:
        head = part.shape[-1] // 2
        out.append((part[:, :head] / part[:, head:]).astype(BF16))
    return jnp.concatenate(out, axis=1)


def loop(count, body):
    if count == 1:
        body(0)
    else:
        lax.fori_loop(0, count, lambda i, c: (body(i), c)[1], 0)


def large_kernel(
    tiles,
    wet_hbm,
    state,
    w_vqkv,
    w_vout,
    w_hqkv,
    w_hout,
    out,
    wet,
    own,
    halo,
    mixed,
    vqkv,
    vout,
    hqkv,
    hout,
    sems,
    ready,
    send_sems,
    recv_sems,
):
    rows, cols, levels, width = state.shape
    blocks = rows * cols
    me = lax.axis_index("tile")
    right = lax.rem(me + 1, tiles)
    left = lax.rem(me + tiles - 1, tiles)

    barrier = pltpu.get_barrier_semaphore()
    pl.semaphore_signal(barrier, inc=1, device_id={"tile": left}, device_id_type=MESH)

    started = []

    def fetch(src, dst):
        copy = pltpu.make_async_copy(src, dst, sems.at[len(started)])
        copy.start()
        started.append(copy)
        return copy

    sends = [
        pltpu.make_async_remote_copy(
            src_ref=state.at[:, column],
            dst_ref=halo.at[i],
            send_sem=send_sems.at[i],
            recv_sem=recv_sems.at[i],
            device_id={"tile": side},
            device_id_type=MESH,
        )
        for i, (column, side) in enumerate(((cols - 1, right), (0, left)))
    ]

    def send_right():
        pl.semaphore_wait(barrier, 1)
        sends[0].start()
        pl.semaphore_signal(ready, inc=1, device_id={"tile": right}, device_id_type=MESH)

    def send_left():
        pl.semaphore_wait(ready, 1)
        sends[1].start()

    last = me == tiles - 1

    def send_first():
        send_right()
        sends[0].wait_send()

    pl.when(last)(send_first)
    get_state = [fetch(state.at[r], own.at[pl.ds(r * cols, cols)]) for r in range(rows)]
    get_vqkv = [fetch(w_vqkv.at[:, pl.ds(i * width, width)], vqkv.at[i]) for i in range(3)]
    pl.when(jnp.logical_not(last))(send_right)
    get_wet = fetch(wet_hbm, wet)
    get_vout = fetch(w_vout, vout)
    get_hqkv = [fetch(w_hqkv.at[:, pl.ds(i * width, width)], hqkv.at[i]) for i in range(3)]
    get_hout = fetch(w_hout, hout)

    def vertical(tokens):
        count = tokens.shape[0]
        values = tokens.astype(F32)
        factor = inverse_rms(values)
        joined = []
        for i in range(3):
            joined.append(dot(tokens, vqkv[i]))
        row = lax.broadcasted_iota(jnp.int32, (count, count), 0) // levels
        col = lax.broadcasted_iota(jnp.int32, (count, count), 1) // levels
        query, keys = unit_heads(joined[0], factor), unit_heads(joined[1], factor)
        context = contexts(weigh(query, keys, value_heads(joined[2], factor), row == col))
        return (values + dot(context, vout[...])).astype(BF16)

    group = max(1, min(blocks, ROWS // levels))
    for copy in get_state:
        copy.wait()
    pl.when(me != 0)(send_left)
    for copy in get_vqkv:
        copy.wait()
    get_vout.wait()

    def own_step(i):
        picked = pl.ds(i * group, group)
        tokens = own[picked].reshape(group * levels, width)
        mixed[picked] = vertical(tokens).reshape(group, levels, width)

    loop(blocks // group, own_step)

    pl.when(me == 0)(send_left)

    for copy in get_hqkv:
        copy.wait()
    get_wet.wait()

    step = min(levels, ROWS // blocks)
    n_own = blocks * step

    key_block = lax.broadcasted_iota(jnp.int32, (1, n_own), 1) // step
    wet_key = jnp.zeros((1, n_own), jnp.int32)
    for b in range(blocks):
        wet_key = jnp.where(key_block == b, wet[me * blocks + b], wet_key)
    row_id = lax.broadcasted_iota(jnp.int32, (n_own, n_own), 0)
    key_id = lax.broadcasted_iota(jnp.int32, (n_own, n_own), 1)
    near = jnp.abs(row_id // step % cols - key_id // step % cols) <= 1
    counted = jnp.logical_or(wet_key > 0, row_id // step == key_block)
    own_mask = (row_id % step == key_id % step) & near & counted

    edges = [r * cols + c for r in range(rows) for c in (0, cols - 1)]
    n_edge = len(edges) * step
    row_id = lax.broadcasted_iota(jnp.int32, (n_edge, 2 * step), 0)
    key_id = lax.broadcasted_iota(jnp.int32, (n_edge, 2 * step), 1)
    halo_mask = (row_id % step == key_id % step) & (row_id // step % 2 == key_id // step)

    def edge_rows(values):
        return jnp.concatenate([values[b * step : (b + 1) * step] for b in edges], axis=0)

    def inner_rows(values):
        spans = [((r * cols + 1) * step, (r * cols + cols - 1) * step) for r in range(rows)]
        return jnp.concatenate([values[first:end] for first, end in spans], axis=0)

    def among_own(i):
        picked = pl.ds(i * step, step)
        tokens = mixed[pl.ds(0, blocks), picked].reshape(n_own, width)
        values = tokens.astype(F32)
        factor = inverse_rms(values)
        query = unit_heads(dot(tokens, hqkv[0]), factor)
        keys = unit_heads(dot(tokens, hqkv[1]), factor)
        value = value_heads(dot(tokens, hqkv[2]), factor)
        parts = weigh(query, keys, value, own_mask)
        context = contexts([inner_rows(p) for p in parts])
        updated = (inner_rows(values) + dot(context, hout[...])).astype(BF16)
        updated = updated.reshape(rows, cols - 2, step, width)
        for r in range(rows):
            out[pl.ds(r * cols + 1, cols - 2), picked] = updated[r]
        query = [edge_rows(q) for q in query]
        return edge_rows(values), query, [edge_rows(p) for p in parts]

    def with_halo(i, beside, values, query, parts):
        picked = pl.ds(i * step, step)
        factor = inverse_rms(beside.astype(F32))
        keys = unit_heads(dot(beside, hqkv[1]), factor)
        value = value_heads(dot(beside, hqkv[2]), factor)
        more = weigh(query, keys, value, halo_mask)
        context = contexts([a + b for a, b in zip(parts, more)])
        updated = (values + dot(context, hout[...])).astype(BF16)
        for e, b in enumerate(edges):
            out[b, picked] = updated[e * step : (e + 1) * step]

    get_hout.wait()
    for i, copy in enumerate(sends):
        copy.wait_recv()
        block = (left * blocks + cols - 1, right * blocks)[i]
        picked_halo = jnp.where(wet[block] > 0, halo[i, 0], halo[i, 1])
        mixed[blocks + i] = vertical(picked_halo)

    def level_step(i):
        beside = mixed[pl.ds(blocks, 2), pl.ds(i * step, step)]
        with_halo(i, beside.reshape(2 * step, width), *among_own(i))

    loop(levels // step, level_step)
    pl.when(jnp.logical_not(last))(sends[0].wait_send)
    sends[1].wait_send()


def lanes(values, h):
    head = values.shape[-1] // HEADS
    return values[..., h * head : (h + 1) * head]


def square_means(values):
    return [jnp.mean(lanes(values, h) * lanes(values, h), axis=-1, keepdims=True) for h in range(HEADS)]


def small_kernel(
    tiles,
    wet_hbm,
    state,
    w_vqkv,
    w_vout,
    w_hqkv,
    w_hout,
    out,
    wet,
    own,
    halo,
    edge_base,
    edge_query,
    edge_total,
    edge_share,
    joint,
    vout,
    hqkv,
    hout,
    folded,
    ready,
    recv_sems,
):
    rows, cols, levels, width = state.shape
    blocks = rows * cols
    head = width // HEADS
    count = blocks * levels
    scale = 1.0 / math.sqrt(head)
    me = lax.axis_index("tile")
    last = me == tiles - 1
    right = jnp.where(last, 0, me + 1)
    left = jnp.where(me == 0, tiles - 1, me - 1)

    barrier = pltpu.get_barrier_semaphore()
    pl.semaphore_signal(barrier, inc=1, device_id={"tile": left}, device_id_type=MESH)

    def in_scope(sems, send_sems):
        third = [pl.ds(i * width, width) for i in range(4)]
        spans = [pl.ds(p * width // PIECES, width // PIECES) for p in range(PIECES)]

        def halo_copy(i, span, sem, column, side):
            return pltpu.make_async_remote_copy(
                src_ref=state.at[:, column, :, span],
                dst_ref=halo.at[i, :, :, span],
                send_sem=send_sems.at[i],
                recv_sem=recv_sems.at[sem],
                device_id={"tile": side},
                device_id_type=MESH,
            )

        full = pl.ds(0, width)
        rightward = [halo_copy(0, span, p, cols - 1, right) for p, span in enumerate(spans)]
        leftward = halo_copy(1, full, len(spans), 0, left)

        def wait_sent(i):
            halo_copy(i, full, 0, 0, right).wait_send()

        def send_right():
            pl.semaphore_wait(barrier, 1)
            for copy in rightward:
                copy.start()
            pl.semaphore_signal(ready, inc=1, device_id={"tile": right}, device_id_type=MESH)

        def send_left():
            pl.semaphore_wait(ready, 1)
            leftward.start()

        def send_first():
            send_right()
            wait_sent(0)

        started = []

        def fetch(src, dst):
            copy = pltpu.make_async_copy(src, dst, sems.at[len(started)])
            copy.start()
            started.append(copy)
            return copy

        pl.when(last)(send_first)
        get_state = [fetch(state.at[r], own.at[pl.ds(r * cols, cols)]) for r in range(rows)]
        get_vqkv = [fetch(w_vqkv.at[:, third[i]], joint.at[:, third[i]]) for i in range(3)]
        pl.when(jnp.logical_not(last))(send_right)
        get_wet = fetch(wet_hbm, wet)
        get_vout = fetch(w_vout, vout)
        get_hqkv = [fetch(w_hqkv.at[:, third[i]], hqkv.at[:, third[i]]) for i in range(2)]
        get_hqkv.append(fetch(w_hqkv.at[:, third[2]], joint.at[:, third[3]]))
        get_hout = fetch(w_hout, hout)

        for copy in get_state:
            copy.wait()
        tokens = own[...].reshape(count, width)
        values = tokens.astype(F32)
        factor = inverse_rms(values)
        joined = []
        for i in range(3):
            get_vqkv[i].wait()
            joined.append(dot(tokens, joint[:, third[i]]))
            if i == 0:
                pl.when(me != 0)(send_left)
        row = lax.broadcasted_iota(jnp.int32, (count, count), 0)
        col = lax.broadcasted_iota(jnp.int32, (count, count), 1)
        query, keys = unit_heads(joined[0], factor), unit_heads(joined[1], factor)
        same_block = row // levels == col // levels
        context = contexts(weigh(query, keys, value_heads(joined[2], factor), same_block))
        get_vout.wait()
        tokens = (values + dot(context, vout[...])).astype(BF16)

        for copy in get_hqkv:
            copy.wait()
        get_wet.wait()
        key_block = lax.broadcasted_iota(jnp.int32, (1, count), 1) // levels
        wet_key = jnp.zeros((1, count), jnp.int32)
        for b in range(blocks):
            wet_key = jnp.where(key_block == b, wet[me * blocks + b], wet_key)
        near = jnp.abs(row // levels % cols - col // levels % cols) <= 1
        counted = jnp.logical_or(wet_key > 0, row // levels == key_block)
        own_mask = (row % levels == col % levels) & near & counted
        values = tokens.astype(F32)
        factor = inverse_rms(values)
        query = unit_heads(dot(tokens, hqkv[:, third[0]]), factor)
        keys = unit_heads(dot(tokens, hqkv[:, third[1]]), factor)
        value = value_heads(dot(tokens, joint[:, third[3]]), factor)
        parts = weigh(query, keys, value, own_mask)

        def block_rows(array, first, number):
            return array[first * levels : (first + number) * levels]

        def inner_rows(array):
            return jnp.concatenate([block_rows(array, r * cols + 1, cols - 2) for r in range(rows)], axis=0)

        get_hout.wait()
        context = contexts([inner_rows(p) for p in parts])
        updated = (inner_rows(values) + dot(context, hout[...])).astype(BF16)
        updated = updated.reshape(rows, cols - 2, levels, width)
        for r in range(rows):
            out[pl.ds(r * cols + 1, cols - 2)] = updated[r]

        edges = [(side, r, r * cols + side * (cols - 1)) for side in range(2) for r in range(rows)]
        bases = [block_rows(values, b, 1) for _, _, b in edges]
        for h in range(HEADS):
            sums = jnp.concatenate([block_rows(parts[h], b, 1) for _, _, b in edges], axis=0)
            shares = dot((sums[:, :head] / sums[:, head:]).astype(BF16), hout[pl.ds(h * head, head)])
            for e, (side, r, b) in enumerate(edges):
                edge_query[side, r, h] = block_rows(query[h], b, 1).astype(F32) * scale
                edge_total[side, r, h] = block_rows(parts[h], b, 1)[:, head:]
                share = block_rows(shares, e, 1)
                edge_share[side, r, h] = share
                bases[e] = bases[e] + share
        for e, (side, r, b) in enumerate(edges):
            edge_base[side, r] = bases[e]

        folded[...] = dot(vout[...], joint[:, third[3]]).astype(BF16)

        def beside(step):
            side = jnp.where(me == 0, 1 - step, step)
            block = jnp.where(side == 0, left * blocks + cols - 1, right * blocks)
            first = wet[block] > 0
            pieces = []
            pl.when(side == 1)(leftward.wait_recv)
            for p, span in enumerate(spans):
                pl.when(side == 0)(rightward[p].wait_recv)
                pieces.append(jnp.where(first, halo[side, 0, :, span], halo[side, 1, :, span]))
                product = dot(pieces[p], joint[span])
                joined = product if p == 0 else joined + product
            tokens = jnp.concatenate(pieces, axis=1)
            joined = [joined[:, i * width : (i + 1) * width] for i in range(4)]
            next_value = joined[3]
            values = tokens.astype(F32)
            factor = inverse_rms(values)
            query, keys, value = [j * factor for j in joined[:3]]
            query_mean, key_mean = square_means(query), square_means(keys)
            value = value.astype(BF16)
            expon = []
            for h in range(HEADS):
                q, k = lanes(query, h), lanes(keys, h)
                scores = lax.dot_general(
                    q.astype(BF16), k.astype(BF16), (((1,), (1,)), ((), ())), preferred_element_type=F32
                )
                by_key = jnp.broadcast_to(lax.rsqrt(key_mean[h] + EPSILON), (levels, head))
                by_key = jnp.transpose(by_key)[:levels]
                scores = scores * (lax.rsqrt(query_mean[h] + EPSILON) * scale) * by_key
                expon.append(jnp.exp(scores))
            mixed = values
            value = [lanes(value, h) for h in range(HEADS)]
            rows_of = [pl.ds(h * head, head) for h in range(HEADS)]
            projected = [dot(value[h], vout[rows_of[h]]).astype(BF16) for h in range(HEADS)]
            twice = [dot(value[h], folded[rows_of[h]]).astype(BF16) for h in range(HEADS)]
            inverse = [1.0 / jnp.sum(e, axis=-1, keepdims=True) for e in expon]
            expon = [e.astype(BF16) for e in expon]
            for h in range(HEADS):
                mixed = mixed + dot(expon[h], projected[h]) * inverse[h]
            for h in range(HEADS):
                next_value = next_value + dot(expon[h], twice[h]) * inverse[h]
            value = next_value.astype(BF16)
            keys = dot(mixed.astype(BF16), hqkv[:, third[1]])
            factor = inverse_rms(mixed)
            projected = [dot(lanes(value, h), hout[rows_of[h]]) for h in range(HEADS)]
            unit = [factor * lax.rsqrt(factor * factor * mean + EPSILON) for mean in square_means(keys)]
            projected = [p * factor for p in projected]
            for r in range(rows):
                updated = edge_base[side, r]
                for h in range(HEADS):
                    scores = jnp.sum(edge_query[side, r, h] * lanes(keys, h), axis=-1, keepdims=True)
                    expon = jnp.exp(scores * unit[h])
                    weight = expon / (edge_total[side, r, h] + expon)
                    weight = jnp.concatenate([weight] * HEADS, axis=1)
                    updated = updated + weight * (projected[h] - edge_share[side, r, h])
                out[r * cols + side * (cols - 1)] = updated.astype(BF16)

        pl.when(me == 0)(send_left)
        loop(2, beside)

        pl.when(jnp.logical_not(last))(functools.partial(wait_sent, 0))
        wait_sent(1)

    pl.run_scoped(in_scope, pltpu.SemaphoreType.DMA((9 + rows,)), pltpu.SemaphoreType.DMA((2,)))


def on_device(tiles, state, wet, w_vqkv, w_vout, w_hqkv, w_hout):
    blocks, levels, width = state.shape
    rows = blocks // CB
    grid = state.reshape(rows, CB, levels, width)
    operands = (wet, grid, w_vqkv, w_vout, w_hqkv, w_hout)
    operands = [pltpu.with_memory_space_constraint(x, pltpu.HBM) for x in operands]
    any_space = pl.BlockSpec(memory_space=pl.ANY)
    head = width // HEADS
    whole = pltpu.VMEM((width, width), BF16)
    if blocks * levels <= ROWS:
        kernel = small_kernel
        semaphores = [pltpu.SemaphoreType.REGULAR, pltpu.SemaphoreType.DMA((PIECES + 1,))]
        scratch = [
            pltpu.VMEM((2, rows, levels, width), F32),
            pltpu.VMEM((2, rows, HEADS, levels, head), F32),
            pltpu.VMEM((2, rows, HEADS, levels, head), F32),
            pltpu.VMEM((2, rows, HEADS, levels, width), F32),
            pltpu.VMEM((width, 4 * width), BF16),
            whole,
            pltpu.VMEM((width, 2 * width), BF16),
            whole,
            whole,
        ]
    else:
        kernel = large_kernel
        two = pltpu.SemaphoreType.DMA((2,))
        semaphores = [pltpu.SemaphoreType.DMA((9 + rows,)), pltpu.SemaphoreType.REGULAR, two, two]
        three = pltpu.VMEM((3, width, width), BF16)
        scratch = [pltpu.VMEM((blocks + 2, levels, width), BF16), three, whole, three, whole]
    return pl.pallas_call(
        functools.partial(kernel, tiles),
        out_shape=jax.ShapeDtypeStruct((blocks, levels, width), BF16),
        in_specs=[any_space] * 6,
        out_specs=pl.BlockSpec(memory_space=pltpu.VMEM),
        scratch_shapes=[
            pltpu.SMEM(wet.shape, jnp.int32),
            pltpu.VMEM((blocks, levels, width), BF16),
            pltpu.VMEM((2, rows, levels, width), BF16),
            *scratch,
            *semaphores,
        ],
        compiler_params=pltpu.CompilerParams(
            collective_id=0, has_side_effects=True, vmem_limit_bytes=48 * 1024 * 1024
        ),
    )(*operands)


def solution(mesh):
    in_specs = (P(("grp", "tile"), None, None), P(), P(), P(), P(), P())
    out_specs = P(("grp", "tile"), None, None)
    return jax.shard_map(
        functools.partial(on_device, mesh.shape["tile"]),
        mesh=mesh,
        in_specs=in_specs,
        out_specs=out_specs,
        check_vma=False,
    )
```

```python
import functools
import math

import jax
import jax.numpy as jnp
from jax import lax
from jax.experimental import pallas as pl
from jax.experimental.pallas import tpu as pltpu
from jax.sharding import PartitionSpec as P

HEADS = 4
CB = 4
ROWS = 128
PIECES = 4
EPSILON = 1e-06
MESH = pl.DeviceIdType.MESH
BF16 = jnp.bfloat16
F32 = jnp.float32


def inverse_rms(values):
    return lax.rsqrt(jnp.mean(values * values, axis=-1, keepdims=True) + EPSILON)


def dot(a, b):
    return jnp.dot(a, b, preferred_element_type=F32)


def unit_heads(raw, factor):
    head = raw.shape[-1] // HEADS
    square = factor * factor
    out = []
    for h in range(HEADS):
        part = raw[:, h * head : (h + 1) * head]
        mean = jnp.mean(part * part, axis=-1, keepdims=True)
        out.append((part * (factor * lax.rsqrt(mean * square + EPSILON))).astype(BF16))
    return out


def value_heads(raw, factor):
    head = raw.shape[-1] // HEADS
    values = (raw * factor).astype(BF16)
    ones = jnp.ones((values.shape[0], head), BF16)
    return [
        jnp.concatenate([values[:, h * head : (h + 1) * head], ones], axis=1)
        for h in range(HEADS)
    ]


def weigh(query, keys, values, mask):
    parts = []
    for q, k, v in zip(query, keys, values):
        scale = 1.0 / math.sqrt(q.shape[-1])
        scores = lax.dot_general(q, k, (((1,), (1,)), ((), ())), preferred_element_type=F32)
        expon = jnp.where(mask, jnp.exp(scores * scale), 0.0).astype(BF16)
        parts.append(dot(expon, v))
    return parts


def contexts(parts):
    out = []
    for part in parts:
        head = part.shape[-1] // 2
        out.append((part[:, :head] / part[:, head:]).astype(BF16))
    return jnp.concatenate(out, axis=1)


def loop(count, body):
    if count == 1:
        body(0)
    else:
        lax.fori_loop(0, count, lambda i, c: (body(i), c)[1], 0)


def large_kernel(
    tiles,
    wet_hbm,
    state,
    w_vqkv,
    w_vout,
    w_hqkv,
    w_hout,
    out,
    wet,
    own,
    halo,
    mixed,
    vqkv,
    vout,
    hqkv,
    hout,
    sems,
    ready,
    send_sems,
    recv_sems,
):
    rows, cols, levels, width = state.shape
    blocks = rows * cols
    me = lax.axis_index("tile")
    right = lax.rem(me + 1, tiles)
    left = lax.rem(me + tiles - 1, tiles)

    barrier = pltpu.get_barrier_semaphore()
    pl.semaphore_signal(barrier, inc=1, device_id={"tile": left}, device_id_type=MESH)

    started = []

    def fetch(src, dst):
        copy = pltpu.make_async_copy(src, dst, sems.at[len(started)])
        copy.start()
        started.append(copy)
        return copy

    sends = [
        pltpu.make_async_remote_copy(
            src_ref=state.at[:, column],
            dst_ref=halo.at[i],
            send_sem=send_sems.at[i],
            recv_sem=recv_sems.at[i],
            device_id={"tile": side},
            device_id_type=MESH,
        )
        for i, (column, side) in enumerate(((cols - 1, right), (0, left)))
    ]

    def send_right():
        pl.semaphore_wait(barrier, 1)
        sends[0].start()
        pl.semaphore_signal(ready, inc=1, device_id={"tile": right}, device_id_type=MESH)

    def send_left():
        pl.semaphore_wait(ready, 1)
        sends[1].start()

    last = me == tiles - 1

    def send_first():
        send_right()
        sends[0].wait_send()

    pl.when(last)(send_first)
    get_state = [fetch(state.at[r], own.at[pl.ds(r * cols, cols)]) for r in range(rows)]
    get_vqkv = [fetch(w_vqkv.at[:, pl.ds(i * width, width)], vqkv.at[i]) for i in range(3)]
    pl.when(jnp.logical_not(last))(send_right)
    get_wet = fetch(wet_hbm, wet)
    get_vout = fetch(w_vout, vout)
    get_hqkv = [fetch(w_hqkv.at[:, pl.ds(i * width, width)], hqkv.at[i]) for i in range(3)]
    get_hout = fetch(w_hout, hout)

    def vertical(tokens):
        count = tokens.shape[0]
        values = tokens.astype(F32)
        factor = inverse_rms(values)
        joined = []
        for i in range(3):
            joined.append(dot(tokens, vqkv[i]))
        row = lax.broadcasted_iota(jnp.int32, (count, count), 0) // levels
        col = lax.broadcasted_iota(jnp.int32, (count, count), 1) // levels
        query, keys = unit_heads(joined[0], factor), unit_heads(joined[1], factor)
        context = contexts(weigh(query, keys, value_heads(joined[2], factor), row == col))
        return (values + dot(context, vout[...])).astype(BF16)

    group = max(1, min(blocks, ROWS // levels))
    for copy in get_state:
        copy.wait()
    pl.when(me != 0)(send_left)
    for copy in get_vqkv:
        copy.wait()
    get_vout.wait()

    def own_step(i):
        picked = pl.ds(i * group, group)
        tokens = own[picked].reshape(group * levels, width)
        mixed[picked] = vertical(tokens).reshape(group, levels, width)

    loop(blocks // group, own_step)

    pl.when(me == 0)(send_left)

    for copy in get_hqkv:
        copy.wait()
    get_wet.wait()

    step = min(levels, ROWS // blocks)
    n_own = blocks * step

    key_block = lax.broadcasted_iota(jnp.int32, (1, n_own), 1) // step
    wet_key = jnp.zeros((1, n_own), jnp.int32)
    for b in range(blocks):
        wet_key = jnp.where(key_block == b, wet[me * blocks + b], wet_key)
    row_id = lax.broadcasted_iota(jnp.int32, (n_own, n_own), 0)
    key_id = lax.broadcasted_iota(jnp.int32, (n_own, n_own), 1)
    near = jnp.abs(row_id // step % cols - key_id // step % cols) <= 1
    counted = jnp.logical_or(wet_key > 0, row_id // step == key_block)
    own_mask = (row_id % step == key_id % step) & near & counted

    edges = [r * cols + c for r in range(rows) for c in (0, cols - 1)]
    n_edge = len(edges) * step
    row_id = lax.broadcasted_iota(jnp.int32, (n_edge, 2 * step), 0)
    key_id = lax.broadcasted_iota(jnp.int32, (n_edge, 2 * step), 1)
    halo_mask = (row_id % step == key_id % step) & (row_id // step % 2 == key_id // step)

    def edge_rows(values):
        return jnp.concatenate([values[b * step : (b + 1) * step] for b in edges], axis=0)

    def inner_rows(values):
        spans = [((r * cols + 1) * step, (r * cols + cols - 1) * step) for r in range(rows)]
        return jnp.concatenate([values[first:end] for first, end in spans], axis=0)

    def among_own(i):
        picked = pl.ds(i * step, step)
        tokens = mixed[pl.ds(0, blocks), picked].reshape(n_own, width)
        values = tokens.astype(F32)
        factor = inverse_rms(values)
        query = unit_heads(dot(tokens, hqkv[0]), factor)
        keys = unit_heads(dot(tokens, hqkv[1]), factor)
        value = value_heads(dot(tokens, hqkv[2]), factor)
        parts = weigh(query, keys, value, own_mask)
        context = contexts([inner_rows(p) for p in parts])
        updated = (inner_rows(values) + dot(context, hout[...])).astype(BF16)
        updated = updated.reshape(rows, cols - 2, step, width)
        for r in range(rows):
            out[pl.ds(r * cols + 1, cols - 2), picked] = updated[r]
        query = [edge_rows(q) for q in query]
        return edge_rows(values), query, [edge_rows(p) for p in parts]

    def with_halo(i, beside, values, query, parts):
        picked = pl.ds(i * step, step)
        factor = inverse_rms(beside.astype(F32))
        keys = unit_heads(dot(beside, hqkv[1]), factor)
        value = value_heads(dot(beside, hqkv[2]), factor)
        more = weigh(query, keys, value, halo_mask)
        context = contexts([a + b for a, b in zip(parts, more)])
        updated = (values + dot(context, hout[...])).astype(BF16)
        for e, b in enumerate(edges):
            out[b, picked] = updated[e * step : (e + 1) * step]

    get_hout.wait()
    for i, copy in enumerate(sends):
        copy.wait_recv()
        block = (left * blocks + cols - 1, right * blocks)[i]
        picked_halo = jnp.where(wet[block] > 0, halo[i, 0], halo[i, 1])
        mixed[blocks + i] = vertical(picked_halo)

    def level_step(i):
        beside = mixed[pl.ds(blocks, 2), pl.ds(i * step, step)]
        with_halo(i, beside.reshape(2 * step, width), *among_own(i))

    loop(levels // step, level_step)
    pl.when(jnp.logical_not(last))(sends[0].wait_send)
    sends[1].wait_send()


def lanes(values, h):
    head = values.shape[-1] // HEADS
    return values[..., h * head : (h + 1) * head]


def square_means(values):
    return [jnp.mean(lanes(values, h) * lanes(values, h), axis=-1, keepdims=True) for h in range(HEADS)]


def small_kernel(
    tiles,
    wet_hbm,
    state,
    w_vqkv,
    w_vout,
    w_hqkv,
    w_hout,
    out,
    wet,
    own,
    halo,
    edge_base,
    edge_query,
    edge_total,
    edge_share,
    joint,
    vout,
    hqkv,
    hout,
    folded,
    ready,
    recv_sems,
):
    rows, cols, levels, width = state.shape
    blocks = rows * cols
    head = width // HEADS
    count = blocks * levels
    scale = 1.0 / math.sqrt(head)
    me = lax.axis_index("tile")
    last = me == tiles - 1
    right = jnp.where(last, 0, me + 1)
    left = jnp.where(me == 0, tiles - 1, me - 1)

    barrier = pltpu.get_barrier_semaphore()
    pl.semaphore_signal(barrier, inc=1, device_id={"tile": left}, device_id_type=MESH)

    def in_scope(sems, send_sems):
        third = [pl.ds(i * width, width) for i in range(4)]
        spans = [pl.ds(p * width // PIECES, width // PIECES) for p in range(PIECES)]

        def halo_copy(i, span, sem, column, side):
            return pltpu.make_async_remote_copy(
                src_ref=state.at[:, column, :, span],
                dst_ref=halo.at[i, :, :, span],
                send_sem=send_sems.at[i],
                recv_sem=recv_sems.at[sem],
                device_id={"tile": side},
                device_id_type=MESH,
            )

        full = pl.ds(0, width)
        rightward = [halo_copy(0, span, p, cols - 1, right) for p, span in enumerate(spans)]
        leftward = halo_copy(1, full, len(spans), 0, left)

        def wait_sent(i):
            halo_copy(i, full, 0, 0, right).wait_send()

        def send_right():
            pl.semaphore_wait(barrier, 1)
            for copy in rightward:
                copy.start()
            pl.semaphore_signal(ready, inc=1, device_id={"tile": right}, device_id_type=MESH)

        def send_left():
            pl.semaphore_wait(ready, 1)
            leftward.start()

        def send_first():
            send_right()
            wait_sent(0)

        started = []

        def fetch(src, dst):
            copy = pltpu.make_async_copy(src, dst, sems.at[len(started)])
            copy.start()
            started.append(copy)
            return copy

        pl.when(last)(send_first)
        get_state = [fetch(state.at[r], own.at[pl.ds(r * cols, cols)]) for r in range(rows)]
        get_vqkv = [fetch(w_vqkv.at[:, third[i]], joint.at[:, third[i]]) for i in range(3)]
        pl.when(jnp.logical_not(last))(send_right)
        get_wet = fetch(wet_hbm, wet)
        get_vout = fetch(w_vout, vout)
        get_hqkv = [fetch(w_hqkv.at[:, third[i]], hqkv.at[:, third[i]]) for i in range(2)]
        get_hqkv.append(fetch(w_hqkv.at[:, third[2]], joint.at[:, third[3]]))
        get_hout = fetch(w_hout, hout)

        for copy in get_state:
            copy.wait()
        tokens = own[...].reshape(count, width)
        values = tokens.astype(F32)
        factor = inverse_rms(values)
        joined = []
        for i in range(3):
            get_vqkv[i].wait()
            joined.append(dot(tokens, joint[:, third[i]]))
            if i == 0:
                pl.when(me != 0)(send_left)
        row = lax.broadcasted_iota(jnp.int32, (count, count), 0)
        col = lax.broadcasted_iota(jnp.int32, (count, count), 1)
        query, keys = unit_heads(joined[0], factor), unit_heads(joined[1], factor)
        same_block = row // levels == col // levels
        context = contexts(weigh(query, keys, value_heads(joined[2], factor), same_block))
        get_vout.wait()
        tokens = (values + dot(context, vout[...])).astype(BF16)

        for copy in get_hqkv:
            copy.wait()
        get_wet.wait()
        key_block = lax.broadcasted_iota(jnp.int32, (1, count), 1) // levels
        wet_key = jnp.zeros((1, count), jnp.int32)
        for b in range(blocks):
            wet_key = jnp.where(key_block == b, wet[me * blocks + b], wet_key)
        near = jnp.abs(row // levels % cols - col // levels % cols) <= 1
        counted = jnp.logical_or(wet_key > 0, row // levels == key_block)
        own_mask = (row % levels == col % levels) & near & counted
        values = tokens.astype(F32)
        factor = inverse_rms(values)
        query = unit_heads(dot(tokens, hqkv[:, third[0]]), factor)
        keys = unit_heads(dot(tokens, hqkv[:, third[1]]), factor)
        value = value_heads(dot(tokens, joint[:, third[3]]), factor)
        parts = weigh(query, keys, value, own_mask)

        def block_rows(array, first, number):
            return array[first * levels : (first + number) * levels]

        def inner_rows(array):
            return jnp.concatenate([block_rows(array, r * cols + 1, cols - 2) for r in range(rows)], axis=0)

        get_hout.wait()
        context = contexts([inner_rows(p) for p in parts])
        updated = (inner_rows(values) + dot(context, hout[...])).astype(BF16)
        updated = updated.reshape(rows, cols - 2, levels, width)
        for r in range(rows):
            out[pl.ds(r * cols + 1, cols - 2)] = updated[r]

        edges = [(side, r, r * cols + side * (cols - 1)) for side in range(2) for r in range(rows)]
        bases = [block_rows(values, b, 1) for _, _, b in edges]
        for h in range(HEADS):
            sums = jnp.concatenate([block_rows(parts[h], b, 1) for _, _, b in edges], axis=0)
            shares = dot((sums[:, :head] / sums[:, head:]).astype(BF16), hout[pl.ds(h * head, head)])
            for e, (side, r, b) in enumerate(edges):
                edge_query[side, r, h] = block_rows(query[h], b, 1).astype(F32) * scale
                edge_total[side, r, h] = block_rows(parts[h], b, 1)[:, head:]
                share = block_rows(shares, e, 1)
                edge_share[side, r, h] = share
                bases[e] = bases[e] + share
        for e, (side, r, b) in enumerate(edges):
            edge_base[side, r] = bases[e]

        folded[...] = dot(vout[...], joint[:, third[3]]).astype(BF16)

        def beside(step):
            side = jnp.where(me == 0, 1 - step, step)
            block = jnp.where(side == 0, left * blocks + cols - 1, right * blocks)
            first = wet[block] > 0
            pieces = []
            pl.when(side == 1)(leftward.wait_recv)
            for p, span in enumerate(spans):
                pl.when(side == 0)(rightward[p].wait_recv)
                pieces.append(jnp.where(first, halo[side, 0, :, span], halo[side, 1, :, span]))
                product = dot(pieces[p], joint[span])
                joined = product if p == 0 else joined + product
            tokens = jnp.concatenate(pieces, axis=1)
            joined = [joined[:, i * width : (i + 1) * width] for i in range(4)]
            next_value = joined[3]
            values = tokens.astype(F32)
            factor = inverse_rms(values)
            query, keys = joined[:2]
            value = joined[2] * factor
            squared = factor * factor
            key_mean, query_mean = square_means(keys), square_means(query)
            value = value.astype(BF16)
            expon = []
            for h in range(HEADS):
                q, k = lanes(query, h), lanes(keys, h)
                scores = lax.dot_general(
                    q.astype(BF16), k.astype(BF16), (((1,), (1,)), ((), ())), preferred_element_type=F32
                )
                by_key = jnp.broadcast_to(factor * lax.rsqrt(key_mean[h] * squared + EPSILON), (levels, head))
                by_key = jnp.transpose(by_key)[:levels]
                by_query = (factor * scale) * lax.rsqrt(query_mean[h] * squared + EPSILON)
                scores = scores * (by_query * by_key)
                expon.append(jnp.exp(scores))
            mixed = values
            value = [lanes(value, h) for h in range(HEADS)]
            rows_of = [pl.ds(h * head, head) for h in range(HEADS)]
            projected = [dot(value[h], vout[rows_of[h]]).astype(BF16) for h in range(HEADS)]
            twice = [dot(value[h], folded[rows_of[h]]).astype(BF16) for h in range(HEADS)]
            inverse = [1.0 / jnp.sum(e, axis=-1, keepdims=True) for e in expon]
            expon = [e.astype(BF16) for e in expon]
            for h in range(HEADS):
                mixed = mixed + dot(expon[h], projected[h]) * inverse[h]
            for h in range(HEADS):
                next_value = next_value + dot(expon[h], twice[h]) * inverse[h]
            value = next_value.astype(BF16)
            keys = dot(mixed.astype(BF16), hqkv[:, third[1]])
            factor = inverse_rms(mixed)
            projected = [dot(lanes(value, h), hout[rows_of[h]]) for h in range(HEADS)]
            unit = [factor * lax.rsqrt(factor * factor * mean + EPSILON) for mean in square_means(keys)]
            projected = [p * factor for p in projected]
            for r in range(rows):
                updated = edge_base[side, r]
                for h in range(HEADS):
                    scores = jnp.sum(edge_query[side, r, h] * lanes(keys, h), axis=-1, keepdims=True)
                    expon = jnp.exp(scores * unit[h])
                    weight = expon / (edge_total[side, r, h] + expon)
                    weight = jnp.concatenate([weight] * HEADS, axis=1)
                    updated = updated + weight * (projected[h] - edge_share[side, r, h])
                out[r * cols + side * (cols - 1)] = updated.astype(BF16)

        pl.when(me == 0)(send_left)
        loop(2, beside)

        pl.when(jnp.logical_not(last))(functools.partial(wait_sent, 0))
        wait_sent(1)

    pl.run_scoped(in_scope, pltpu.SemaphoreType.DMA((9 + rows,)), pltpu.SemaphoreType.DMA((2,)))


def on_device(tiles, state, wet, w_vqkv, w_vout, w_hqkv, w_hout):
    blocks, levels, width = state.shape
    rows = blocks // CB
    grid = state.reshape(rows, CB, levels, width)
    operands = (wet, grid, w_vqkv, w_vout, w_hqkv, w_hout)
    operands = [pltpu.with_memory_space_constraint(x, pltpu.HBM) for x in operands]
    any_space = pl.BlockSpec(memory_space=pl.ANY)
    head = width // HEADS
    whole = pltpu.VMEM((width, width), BF16)
    if blocks * levels <= ROWS:
        kernel = small_kernel
        semaphores = [pltpu.SemaphoreType.REGULAR, pltpu.SemaphoreType.DMA((PIECES + 1,))]
        scratch = [
            pltpu.VMEM((2, rows, levels, width), F32),
            pltpu.VMEM((2, rows, HEADS, levels, head), F32),
            pltpu.VMEM((2, rows, HEADS, levels, head), F32),
            pltpu.VMEM((2, rows, HEADS, levels, width), F32),
            pltpu.VMEM((width, 4 * width), BF16),
            whole,
            pltpu.VMEM((width, 2 * width), BF16),
            whole,
            whole,
        ]
    else:
        kernel = large_kernel
        two = pltpu.SemaphoreType.DMA((2,))
        semaphores = [pltpu.SemaphoreType.DMA((9 + rows,)), pltpu.SemaphoreType.REGULAR, two, two]
        three = pltpu.VMEM((3, width, width), BF16)
        scratch = [pltpu.VMEM((blocks + 2, levels, width), BF16), three, whole, three, whole]
    return pl.pallas_call(
        functools.partial(kernel, tiles),
        out_shape=jax.ShapeDtypeStruct((blocks, levels, width), BF16),
        in_specs=[any_space] * 6,
        out_specs=pl.BlockSpec(memory_space=pltpu.VMEM),
        scratch_shapes=[
            pltpu.SMEM(wet.shape, jnp.int32),
            pltpu.VMEM((blocks, levels, width), BF16),
            pltpu.VMEM((2, rows, levels, width), BF16),
            *scratch,
            *semaphores,
        ],
        compiler_params=pltpu.CompilerParams(
            collective_id=0, has_side_effects=True, vmem_limit_bytes=48 * 1024 * 1024
        ),
    )(*operands)


def solution(mesh):
    in_specs = (P(("grp", "tile"), None, None), P(), P(), P(), P(), P())
    out_specs = P(("grp", "tile"), None, None)
    return jax.shard_map(
        functools.partial(on_device, mesh.shape["tile"]),
        mesh=mesh,
        in_specs=in_specs,
        out_specs=out_specs,
        check_vma=False,
    )
```

```python
import functools
import math

import jax
import jax.numpy as jnp
from jax import lax
from jax.experimental import pallas as pl
from jax.experimental.pallas import tpu as pltpu
from jax.sharding import PartitionSpec as P

HEADS = 4
CB = 4
ROWS = 128
PIECES = 4
EPSILON = 1e-06
MESH = pl.DeviceIdType.MESH
BF16 = jnp.bfloat16
F32 = jnp.float32


def inverse_rms(values):
    return lax.rsqrt(jnp.mean(values * values, axis=-1, keepdims=True) + EPSILON)


def dot(a, b):
    return jnp.dot(a, b, preferred_element_type=F32)


def unit_heads(raw, factor):
    head = raw.shape[-1] // HEADS
    square = factor * factor
    out = []
    for h in range(HEADS):
        part = raw[:, h * head : (h + 1) * head]
        mean = jnp.mean(part * part, axis=-1, keepdims=True)
        out.append((part * (factor * lax.rsqrt(mean * square + EPSILON))).astype(BF16))
    return out


def value_heads(raw, factor):
    head = raw.shape[-1] // HEADS
    values = (raw * factor).astype(BF16)
    ones = jnp.ones((values.shape[0], head), BF16)
    return [
        jnp.concatenate([values[:, h * head : (h + 1) * head], ones], axis=1)
        for h in range(HEADS)
    ]


def weigh(query, keys, values, mask):
    parts = []
    for q, k, v in zip(query, keys, values):
        scale = 1.0 / math.sqrt(q.shape[-1])
        scores = lax.dot_general(q, k, (((1,), (1,)), ((), ())), preferred_element_type=F32)
        expon = jnp.where(mask, jnp.exp(scores * scale), 0.0).astype(BF16)
        parts.append(dot(expon, v))
    return parts


def contexts(parts):
    out = []
    for part in parts:
        head = part.shape[-1] // 2
        out.append((part[:, :head] / part[:, head:]).astype(BF16))
    return jnp.concatenate(out, axis=1)


def loop(count, body):
    if count == 1:
        body(0)
    else:
        lax.fori_loop(0, count, lambda i, c: (body(i), c)[1], 0)


def large_kernel(
    tiles,
    wet_hbm,
    state,
    w_vqkv,
    w_vout,
    w_hqkv,
    w_hout,
    out,
    wet,
    own,
    halo,
    mixed,
    vqkv,
    vout,
    hqkv,
    hout,
    sems,
    ready,
    send_sems,
    recv_sems,
):
    rows, cols, levels, width = state.shape
    blocks = rows * cols
    me = lax.axis_index("tile")
    right = lax.rem(me + 1, tiles)
    left = lax.rem(me + tiles - 1, tiles)

    barrier = pltpu.get_barrier_semaphore()
    pl.semaphore_signal(barrier, inc=1, device_id={"tile": left}, device_id_type=MESH)

    started = []

    def fetch(src, dst):
        copy = pltpu.make_async_copy(src, dst, sems.at[len(started)])
        copy.start()
        started.append(copy)
        return copy

    sends = [
        pltpu.make_async_remote_copy(
            src_ref=state.at[:, column],
            dst_ref=halo.at[i],
            send_sem=send_sems.at[i],
            recv_sem=recv_sems.at[i],
            device_id={"tile": side},
            device_id_type=MESH,
        )
        for i, (column, side) in enumerate(((cols - 1, right), (0, left)))
    ]

    def send_right():
        pl.semaphore_wait(barrier, 1)
        sends[0].start()
        pl.semaphore_signal(ready, inc=1, device_id={"tile": right}, device_id_type=MESH)

    def send_left():
        pl.semaphore_wait(ready, 1)
        sends[1].start()

    last = me == tiles - 1

    def send_first():
        send_right()
        sends[0].wait_send()

    pl.when(last)(send_first)
    get_state = [fetch(state.at[r], own.at[pl.ds(r * cols, cols)]) for r in range(rows)]
    get_vqkv = [fetch(w_vqkv.at[:, pl.ds(i * width, width)], vqkv.at[i]) for i in range(3)]
    pl.when(jnp.logical_not(last))(send_right)
    get_wet = fetch(wet_hbm, wet)
    get_vout = fetch(w_vout, vout)
    get_hqkv = [fetch(w_hqkv.at[:, pl.ds(i * width, width)], hqkv.at[i]) for i in range(3)]
    get_hout = fetch(w_hout, hout)

    def vertical(tokens):
        count = tokens.shape[0]
        values = tokens.astype(F32)
        factor = inverse_rms(values)
        joined = []
        for i in range(3):
            joined.append(dot(tokens, vqkv[i]))
        row = lax.broadcasted_iota(jnp.int32, (count, count), 0) // levels
        col = lax.broadcasted_iota(jnp.int32, (count, count), 1) // levels
        query, keys = unit_heads(joined[0], factor), unit_heads(joined[1], factor)
        context = contexts(weigh(query, keys, value_heads(joined[2], factor), row == col))
        return (values + dot(context, vout[...])).astype(BF16)

    group = max(1, min(blocks, ROWS // levels))
    for copy in get_state:
        copy.wait()
    pl.when(me != 0)(send_left)
    for copy in get_vqkv:
        copy.wait()
    get_vout.wait()

    def own_step(i):
        picked = pl.ds(i * group, group)
        tokens = own[picked].reshape(group * levels, width)
        mixed[picked] = vertical(tokens).reshape(group, levels, width)

    loop(blocks // group, own_step)

    pl.when(me == 0)(send_left)

    for copy in get_hqkv:
        copy.wait()
    get_wet.wait()

    step = min(levels, ROWS // blocks)
    n_own = blocks * step

    key_block = lax.broadcasted_iota(jnp.int32, (1, n_own), 1) // step
    wet_key = jnp.zeros((1, n_own), jnp.int32)
    for b in range(blocks):
        wet_key = jnp.where(key_block == b, wet[me * blocks + b], wet_key)
    row_id = lax.broadcasted_iota(jnp.int32, (n_own, n_own), 0)
    key_id = lax.broadcasted_iota(jnp.int32, (n_own, n_own), 1)
    near = jnp.abs(row_id // step % cols - key_id // step % cols) <= 1
    counted = jnp.logical_or(wet_key > 0, row_id // step == key_block)
    own_mask = (row_id % step == key_id % step) & near & counted

    edges = [r * cols + c for r in range(rows) for c in (0, cols - 1)]
    n_edge = len(edges) * step
    row_id = lax.broadcasted_iota(jnp.int32, (n_edge, 2 * step), 0)
    key_id = lax.broadcasted_iota(jnp.int32, (n_edge, 2 * step), 1)
    halo_mask = (row_id % step == key_id % step) & (row_id // step % 2 == key_id // step)

    def edge_rows(values):
        return jnp.concatenate([values[b * step : (b + 1) * step] for b in edges], axis=0)

    def inner_rows(values):
        spans = [((r * cols + 1) * step, (r * cols + cols - 1) * step) for r in range(rows)]
        return jnp.concatenate([values[first:end] for first, end in spans], axis=0)

    def among_own(i):
        picked = pl.ds(i * step, step)
        tokens = mixed[pl.ds(0, blocks), picked].reshape(n_own, width)
        values = tokens.astype(F32)
        factor = inverse_rms(values)
        query = unit_heads(dot(tokens, hqkv[0]), factor)
        keys = unit_heads(dot(tokens, hqkv[1]), factor)
        value = value_heads(dot(tokens, hqkv[2]), factor)
        parts = weigh(query, keys, value, own_mask)
        context = contexts([inner_rows(p) for p in parts])
        updated = (inner_rows(values) + dot(context, hout[...])).astype(BF16)
        updated = updated.reshape(rows, cols - 2, step, width)
        for r in range(rows):
            out[pl.ds(r * cols + 1, cols - 2), picked] = updated[r]
        query = [edge_rows(q) for q in query]
        return edge_rows(values), query, [edge_rows(p) for p in parts]

    def with_halo(i, beside, values, query, parts):
        picked = pl.ds(i * step, step)
        factor = inverse_rms(beside.astype(F32))
        keys = unit_heads(dot(beside, hqkv[1]), factor)
        value = value_heads(dot(beside, hqkv[2]), factor)
        more = weigh(query, keys, value, halo_mask)
        context = contexts([a + b for a, b in zip(parts, more)])
        updated = (values + dot(context, hout[...])).astype(BF16)
        for e, b in enumerate(edges):
            out[b, picked] = updated[e * step : (e + 1) * step]

    get_hout.wait()
    for i, copy in enumerate(sends):
        copy.wait_recv()
        block = (left * blocks + cols - 1, right * blocks)[i]
        picked_halo = jnp.where(wet[block] > 0, halo[i, 0], halo[i, 1])
        mixed[blocks + i] = vertical(picked_halo)

    def level_step(i):
        beside = mixed[pl.ds(blocks, 2), pl.ds(i * step, step)]
        with_halo(i, beside.reshape(2 * step, width), *among_own(i))

    loop(levels // step, level_step)
    pl.when(jnp.logical_not(last))(sends[0].wait_send)
    sends[1].wait_send()


def lanes(values, h):
    head = values.shape[-1] // HEADS
    return values[..., h * head : (h + 1) * head]


def square_means(values):
    return [jnp.mean(lanes(values, h) * lanes(values, h), axis=-1, keepdims=True) for h in range(HEADS)]


def small_kernel(
    tiles,
    wet_hbm,
    state,
    w_vqkv,
    w_vout,
    w_hqkv,
    w_hout,
    out,
    wet,
    own,
    halo,
    edge_base,
    edge_query,
    edge_total,
    edge_share,
    joint,
    vout,
    hqkv,
    hout,
    folded,
    ready,
    recv_sems,
):
    rows, cols, levels, width = state.shape
    blocks = rows * cols
    head = width // HEADS
    count = blocks * levels
    scale = 1.0 / math.sqrt(head)
    me = lax.axis_index("tile")
    last = me == tiles - 1
    right = jnp.where(last, 0, me + 1)
    left = jnp.where(me == 0, tiles - 1, me - 1)

    barrier = pltpu.get_barrier_semaphore()
    pl.semaphore_signal(barrier, inc=1, device_id={"tile": left}, device_id_type=MESH)

    def in_scope(sems, send_sems):
        third = [pl.ds(i * width, width) for i in range(4)]
        spans = [pl.ds(p * width // PIECES, width // PIECES) for p in range(PIECES)]

        def halo_copy(i, span, sem, column, side):
            return pltpu.make_async_remote_copy(
                src_ref=state.at[:, column, :, span],
                dst_ref=halo.at[i, :, :, span],
                send_sem=send_sems.at[i],
                recv_sem=recv_sems.at[sem],
                device_id={"tile": side},
                device_id_type=MESH,
            )

        full = pl.ds(0, width)
        rightward = [halo_copy(0, span, p, cols - 1, right) for p, span in enumerate(spans)]
        leftward = halo_copy(1, full, len(spans), 0, left)

        def wait_sent(i):
            halo_copy(i, full, 0, 0, right).wait_send()

        def send_right():
            pl.semaphore_wait(barrier, 1)
            for copy in rightward:
                copy.start()
            pl.semaphore_signal(ready, inc=1, device_id={"tile": right}, device_id_type=MESH)

        def send_left():
            pl.semaphore_wait(ready, 1)
            leftward.start()

        def send_first():
            send_right()
            wait_sent(0)

        started = []

        def fetch(src, dst):
            copy = pltpu.make_async_copy(src, dst, sems.at[len(started)])
            copy.start()
            started.append(copy)
            return copy

        pl.when(last)(send_first)
        get_state = [fetch(state.at[r], own.at[pl.ds(r * cols, cols)]) for r in range(rows)]
        get_vqkv = [fetch(w_vqkv.at[:, third[i]], joint.at[:, third[(1, 0, 2)[i]]]) for i in range(3)]
        pl.when(jnp.logical_not(last))(send_right)
        get_wet = fetch(wet_hbm, wet)
        get_vout = fetch(w_vout, vout)
        get_hqkv = [fetch(w_hqkv.at[:, third[i]], hqkv.at[:, third[i]]) for i in range(2)]
        get_hqkv.append(fetch(w_hqkv.at[:, third[2]], joint.at[:, third[3]]))
        get_hout = fetch(w_hout, hout)

        for copy in get_state:
            copy.wait()
        tokens = own[...].reshape(count, width)
        values = tokens.astype(F32)
        factor = inverse_rms(values)
        joined = []
        for i in range(3):
            get_vqkv[i].wait()
            joined.append(dot(tokens, joint[:, third[(1, 0, 2)[i]]]))
            if i == 0:
                pl.when(me != 0)(send_left)
        row = lax.broadcasted_iota(jnp.int32, (count, count), 0)
        col = lax.broadcasted_iota(jnp.int32, (count, count), 1)
        query, keys = unit_heads(joined[0], factor), unit_heads(joined[1], factor)
        same_block = row // levels == col // levels
        context = contexts(weigh(query, keys, value_heads(joined[2], factor), same_block))
        get_vout.wait()
        tokens = (values + dot(context, vout[...])).astype(BF16)

        for copy in get_hqkv:
            copy.wait()
        get_wet.wait()
        key_block = lax.broadcasted_iota(jnp.int32, (1, count), 1) // levels
        wet_key = jnp.zeros((1, count), jnp.int32)
        for b in range(blocks):
            wet_key = jnp.where(key_block == b, wet[me * blocks + b], wet_key)
        near = jnp.abs(row // levels % cols - col // levels % cols) <= 1
        counted = jnp.logical_or(wet_key > 0, row // levels == key_block)
        own_mask = (row % levels == col % levels) & near & counted
        values = tokens.astype(F32)
        factor = inverse_rms(values)
        query = unit_heads(dot(tokens, hqkv[:, third[0]]), factor)
        keys = unit_heads(dot(tokens, hqkv[:, third[1]]), factor)
        value = value_heads(dot(tokens, joint[:, third[3]]), factor)
        parts = weigh(query, keys, value, own_mask)

        def block_rows(array, first, number):
            return array[first * levels : (first + number) * levels]

        def inner_rows(array):
            return jnp.concatenate([block_rows(array, r * cols + 1, cols - 2) for r in range(rows)], axis=0)

        get_hout.wait()
        context = contexts([inner_rows(p) for p in parts])
        updated = (inner_rows(values) + dot(context, hout[...])).astype(BF16)
        updated = updated.reshape(rows, cols - 2, levels, width)
        for r in range(rows):
            out[pl.ds(r * cols + 1, cols - 2)] = updated[r]

        edges = [(side, r, r * cols + side * (cols - 1)) for side in range(2) for r in range(rows)]
        bases = [block_rows(values, b, 1) for _, _, b in edges]
        for h in range(HEADS):
            sums = jnp.concatenate([block_rows(parts[h], b, 1) for _, _, b in edges], axis=0)
            shares = dot((sums[:, :head] / sums[:, head:]).astype(BF16), hout[pl.ds(h * head, head)])
            for e, (side, r, b) in enumerate(edges):
                edge_query[side, r, h] = block_rows(query[h], b, 1).astype(F32) * scale
                edge_total[side, r, h] = block_rows(parts[h], b, 1)[:, head:]
                share = block_rows(shares, e, 1)
                edge_share[side, r, h] = share
                bases[e] = bases[e] + share
        for e, (side, r, b) in enumerate(edges):
            edge_base[side, r] = bases[e]

        folded[...] = dot(vout[...], joint[:, third[3]]).astype(BF16)

        def beside(step):
            side = jnp.where(me == 0, 1 - step, step)
            block = jnp.where(side == 0, left * blocks + cols - 1, right * blocks)
            first = wet[block] > 0
            pieces = []
            pl.when(side == 1)(leftward.wait_recv)
            for p, span in enumerate(spans):
                pl.when(side == 0)(rightward[p].wait_recv)
                pieces.append(jnp.where(first, halo[side, 0, :, span], halo[side, 1, :, span]))
                product = dot(pieces[p], joint[span])
                joined = product if p == 0 else joined + product
            tokens = jnp.concatenate(pieces, axis=1)
            joined = [joined[:, i * width : (i + 1) * width] for i in range(4)]
            next_value = joined[3]
            values = tokens.astype(F32)
            factor = inverse_rms(values)
            keys, query, value = [j * factor for j in joined[:3]]
            query_mean = square_means(query)
            value = value.astype(BF16)
            expon = []
            for h in range(HEADS):
                q, k = lanes(query, h), lanes(keys, h)
                scores = lax.dot_general(
                    q.astype(BF16), k.astype(BF16), (((1,), (1,)), ((), ())), preferred_element_type=F32
                )
                by_key = lax.dot_general(
                    jnp.full((levels, head), 1.0 / head, BF16),
                    (k * k).astype(BF16),
                    (((1,), (1,)), ((), ())),
                    preferred_element_type=F32,
                )
                by_key = lax.rsqrt(by_key + EPSILON)
                scores = scores * (lax.rsqrt(query_mean[h] + EPSILON) * scale) * by_key
                expon.append(jnp.exp(scores))
            mixed = values
            value = [lanes(value, h) for h in range(HEADS)]
            rows_of = [pl.ds(h * head, head) for h in range(HEADS)]
            projected = [dot(value[h], vout[rows_of[h]]).astype(BF16) for h in range(HEADS)]
            twice = [dot(value[h], folded[rows_of[h]]).astype(BF16) for h in range(HEADS)]
            inverse = [1.0 / jnp.sum(e, axis=-1, keepdims=True) for e in expon]
            expon = [e.astype(BF16) for e in expon]
            for h in range(HEADS):
                mixed = mixed + dot(expon[h], projected[h]) * inverse[h]
            for h in range(HEADS):
                next_value = next_value + dot(expon[h], twice[h]) * inverse[h]
            value = next_value.astype(BF16)
            keys = dot(mixed.astype(BF16), hqkv[:, third[1]])
            factor = inverse_rms(mixed)
            projected = [dot(lanes(value, h), hout[rows_of[h]]) for h in range(HEADS)]
            unit = [factor * lax.rsqrt(factor * factor * mean + EPSILON) for mean in square_means(keys)]
            projected = [p * factor for p in projected]
            for r in range(rows):
                updated = edge_base[side, r]
                for h in range(HEADS):
                    scores = jnp.sum(edge_query[side, r, h] * lanes(keys, h), axis=-1, keepdims=True)
                    expon = jnp.exp(scores * unit[h])
                    weight = expon / (edge_total[side, r, h] + expon)
                    weight = jnp.concatenate([weight] * HEADS, axis=1)
                    updated = updated + weight * (projected[h] - edge_share[side, r, h])
                out[r * cols + side * (cols - 1)] = updated.astype(BF16)

        pl.when(me == 0)(send_left)
        loop(2, beside)

        pl.when(jnp.logical_not(last))(functools.partial(wait_sent, 0))
        wait_sent(1)

    pl.run_scoped(in_scope, pltpu.SemaphoreType.DMA((9 + rows,)), pltpu.SemaphoreType.DMA((2,)))


def on_device(tiles, state, wet, w_vqkv, w_vout, w_hqkv, w_hout):
    blocks, levels, width = state.shape
    rows = blocks // CB
    grid = state.reshape(rows, CB, levels, width)
    operands = (wet, grid, w_vqkv, w_vout, w_hqkv, w_hout)
    operands = [pltpu.with_memory_space_constraint(x, pltpu.HBM) for x in operands]
    any_space = pl.BlockSpec(memory_space=pl.ANY)
    head = width // HEADS
    whole = pltpu.VMEM((width, width), BF16)
    if blocks * levels <= ROWS:
        kernel = small_kernel
        semaphores = [pltpu.SemaphoreType.REGULAR, pltpu.SemaphoreType.DMA((PIECES + 1,))]
        scratch = [
            pltpu.VMEM((2, rows, levels, width), F32),
            pltpu.VMEM((2, rows, HEADS, levels, head), F32),
            pltpu.VMEM((2, rows, HEADS, levels, head), F32),
            pltpu.VMEM((2, rows, HEADS, levels, width), F32),
            pltpu.VMEM((width, 4 * width), BF16),
            whole,
            pltpu.VMEM((width, 2 * width), BF16),
            whole,
            whole,
        ]
    else:
        kernel = large_kernel
        two = pltpu.SemaphoreType.DMA((2,))
        semaphores = [pltpu.SemaphoreType.DMA((9 + rows,)), pltpu.SemaphoreType.REGULAR, two, two]
        three = pltpu.VMEM((3, width, width), BF16)
        scratch = [pltpu.VMEM((blocks + 2, levels, width), BF16), three, whole, three, whole]
    return pl.pallas_call(
        functools.partial(kernel, tiles),
        out_shape=jax.ShapeDtypeStruct((blocks, levels, width), BF16),
        in_specs=[any_space] * 6,
        out_specs=pl.BlockSpec(memory_space=pltpu.VMEM),
        scratch_shapes=[
            pltpu.SMEM(wet.shape, jnp.int32),
            pltpu.VMEM((blocks, levels, width), BF16),
            pltpu.VMEM((2, rows, levels, width), BF16),
            *scratch,
            *semaphores,
        ],
        compiler_params=pltpu.CompilerParams(
            collective_id=0, has_side_effects=True, vmem_limit_bytes=48 * 1024 * 1024
        ),
    )(*operands)


def solution(mesh):
    in_specs = (P(("grp", "tile"), None, None), P(), P(), P(), P(), P())
    out_specs = P(("grp", "tile"), None, None)
    return jax.shard_map(
        functools.partial(on_device, mesh.shape["tile"]),
        mesh=mesh,
        in_specs=in_specs,
        out_specs=out_specs,
        check_vma=False,
    )
```
